32 devices in a mesh: epoch: 4 (over x, core), row: 8 (over z, y).
Axes of the slice: x: 2, y: 2, z: 4, core: 2. Of those that a mesh axis runs over, the one named last changes fastest.
Arguments:
- flux_image: float32 [16, 256, 1024], P('epoch', 'row'), may hold values from -8 to 8
- inv_var: float32 [16, 256, 1024], P('epoch', 'row'), may hold values from 0.5 to 4
- pixel_mask: int32 [16, 256, 1024], P('epoch', 'row'), may hold values 0 or 1
- psf_columns: float32 [16, 13], P('epoch'), may hold values from 0.02 to 0.3
- psf_rows: float32 [16, 13], P('epoch'), may hold values from 0.02 to 0.3
- epoch_times: int32 [16], P('epoch'), may hold values from 0 to 63, as said below
- trial_rates: int32 [4, 2], replicated, may hold values from -8 to 8, as said below
Outputs:
- psi_stack: float32 [4, 256, 1024], P('epoch', 'row')
- phi_stack: float32 [4, 256, 1024], P('epoch', 'row')
The draws below stay inside these ranges and needn't reach their ends.
Inputs may be any that keep to these rules, and one draw needn't show every extreme that they name: `epoch_times`: some epoch has time index 0 and some has 63. `trial_rates`: some velocity has row rate 8 and some -8; some has column rate 8 and some -8.
All inputs are finite; a program needn't handle non-finite values. No bound on the sum of `pixel_mask` on one device may be relied on, other than what follows from the above.
Results may differ from the reference program's by a relative error of at most 0.00011.
Values sent between devices are 32-bit elements; how exact they have to be, the bound alone decides.
A program may use at most 64 MiB of HBM per device.

```python
import math
import jax
import jax.numpy as jnp
from jax import lax

COLS = 1024
HALO = 8
PAD = 6
TSPAN = 64
KW = 13
EPOCHS = 16
VELS = 4
ROWS = 256


def draw_epoch_times(key, part):
    base_key, pick_key = jax.random.split(jax.random.fold_in(key, 11))
    values = jax.random.randint(base_key, (EPOCHS,), 0, TSPAN, dtype=jnp.int32)
    order = jax.random.permutation(pick_key, EPOCHS)
    return values.at[order[0]].set(0).at[order[1]].set(TSPAN - 1)


def draw_trial_rates(key, part):
    base_key, pick_key = jax.random.split(jax.random.fold_in(key, 23))
    values = jax.random.randint(base_key, (VELS, 2), -HALO, HALO + 1, dtype=jnp.int32)
    order = jax.random.permutation(pick_key, VELS)
    values = values.at[order[0], 0].set(HALO).at[order[1], 0].set(-HALO)
    return values.at[order[2], 1].set(HALO).at[order[3], 1].set(-HALO)


def with_ends(array, stream_key, low, top_value):
    extent = array.shape
    index_at = [jax.random.randint(jax.random.fold_in(stream_key, axis), (), 0, extent[axis]) for axis in range(len(extent))]
    array = array.at[tuple(index_at)].set(low)
    longest = extent.index(max(extent))
    index_at[longest] = (index_at[longest] + 1) % extent[longest]
    return array.at[tuple(index_at)].set(top_value)


def block_levels(own_key, extent, pieces, smallest, largest):
    def one(dim, blocks):
        heights = jax.random.uniform(jax.random.fold_in(jax.random.fold_in(own_key, 6), dim), (blocks,), jnp.float32, smallest / len(pieces), largest / len(pieces))
        return jnp.repeat(jnp.exp(heights), extent[dim] // blocks).reshape((-1,) + (1,) * (len(extent) - dim - 1))

    loudness = one(*pieces[0])
    for cut in pieces[1:]:
        loudness = loudness * one(*cut)
    return loudness


def normal_values(own_key, shape, width, reach, pieces=(), kind=jnp.bfloat16):
    entries = width * jax.random.normal(own_key, shape, jnp.float32)
    if pieces:
        entries = entries * block_levels(own_key, shape, pieces, -0.22, 0.18)
    return jnp.clip(entries, -reach, reach).astype(kind)


def setup_inputs(seed: int = 0) -> dict:
    key_of = jax.random.split(jax.random.key(seed), 8)
    flux_image = normal_values(key_of[0], (EPOCHS, ROWS, COLS), 1.0, 8.0, ((0, 4), (1, 8)), jnp.float32)
    inv_var = jnp.clip(jnp.exp(math.log(4.0) - 2.0794415 * jax.random.uniform(key_of[1], (EPOCHS, ROWS, COLS), jnp.float32) ** block_levels(key_of[1], (EPOCHS, ROWS, COLS), ((0, 4), (1, 8)), -0.2, 0.2)), 0.5, 4.0)
    pixel_mask = with_ends((jax.random.randint(key_of[2], (EPOCHS, ROWS, COLS), 0, 16) < 15).astype(jnp.int32), jax.random.fold_in(key_of[2], 1), 0, 1)
    psf_columns = jnp.clip(jnp.exp(math.log(0.3) - 2.7080503 * jax.random.uniform(key_of[3], (EPOCHS, KW), jnp.float32) ** block_levels(key_of[3], (EPOCHS, KW), ((0, 4),), -0.2, 0.2)), 0.02, 0.3)
    psf_rows = jnp.clip(jnp.exp(math.log(0.3) - 2.7080503 * jax.random.uniform(key_of[4], (EPOCHS, KW), jnp.float32) ** block_levels(key_of[4], (EPOCHS, KW), ((0, 4),), -0.2, 0.2)), 0.02, 0.3)
    epoch_times = draw_epoch_times(jax.random.fold_in(key_of[7], 71), 0)
    trial_rates = draw_trial_rates(jax.random.fold_in(key_of[7], 71), 0)
    return dict(flux_image=flux_image, inv_var=inv_var, pixel_mask=pixel_mask, psf_columns=psf_columns, psf_rows=psf_rows, epoch_times=epoch_times, trial_rates=trial_rates)


def conv_columns(fields_in, kernel):
    columns = fields_in.shape[3]
    padded = jnp.pad(fields_in, ((0, 0), (0, 0), (0, 0), (PAD, PAD)))
    result = jnp.zeros(fields_in.shape, jnp.float32)
    for tap_index in range(2 * PAD + 1):
        result = result + kernel[:, :, tap_index][:, :, None, None] * padded[:, :, :, tap_index:tap_index + columns]
    return result


def conv_rows_valid(fields_in, kernel):
    out_rows = fields_in.shape[2] - 2 * PAD
    shape_out = (fields_in.shape[0], fields_in.shape[1], out_rows, fields_in.shape[3])
    result = jnp.zeros(shape_out, jnp.float32)
    for tap_index in range(2 * PAD + 1):
        result = result + kernel[:, :, tap_index][:, :, None, None] * fields_in[:, :, tap_index:tap_index + out_rows, :]
    return result


def shifted_sum(padded, row_starts, column_starts, first_vel, how_many, out_rows):
    columns = padded.shape[3] - 2 * HALO
    row_part = lax.dynamic_slice_in_dim(row_starts, first_vel, how_many, 1)
    column_part = lax.dynamic_slice_in_dim(column_starts, first_vel, how_many, 1)

    def add_epoch(epoch_number, running):
        epoch_field = lax.dynamic_index_in_dim(padded, epoch_number, 0, keepdims=False)
        row_now = lax.dynamic_index_in_dim(row_part, epoch_number, 0, keepdims=False)
        column_now = lax.dynamic_index_in_dim(column_part, epoch_number, 0, keepdims=False)

        def take_window(row_begin, column_begin):
            return lax.dynamic_slice(epoch_field, (jnp.int32(0), row_begin, column_begin), (2, out_rows, columns))

        return running + jax.vmap(take_window)(row_now, column_now)

    empty_stack = jnp.zeros((how_many, 2, out_rows, columns), jnp.float32)
    return lax.fori_loop(0, padded.shape[0], add_epoch, empty_stack)


def reference(flux_image, inv_var, pixel_mask, psf_columns, psf_rows, epoch_times, trial_rates):
    weights = inv_var * pixel_mask.astype(jnp.float32)
    fields = jnp.stack([flux_image * weights, weights], axis=1)
    fields = conv_columns(fields, jnp.stack([psf_columns, psf_columns * psf_columns], axis=1))
    row_kernel = jnp.stack([psf_rows, psf_rows * psf_rows], axis=1)
    fields = jnp.pad(fields, ((0, 0), (0, 0), (PAD, PAD), (0, 0)))
    fields = conv_rows_valid(fields, row_kernel)
    padded = jnp.pad(fields, ((0, 0), (0, 0), (HALO, HALO), (HALO, HALO)))
    row_shift = jnp.floor_divide(trial_rates[:, 0][None, :] * epoch_times[:, None], TSPAN).astype(jnp.int32)
    column_shift = jnp.floor_divide(trial_rates[:, 1][None, :] * epoch_times[:, None], TSPAN).astype(jnp.int32)
    stacks = shifted_sum(padded, row_shift + HALO, column_shift + HALO, 0, VELS, ROWS)
    return stacks[:, 0], stacks[:, 1]
```

```python
import functools

import jax
import jax.numpy as jnp
from jax import lax
from jax.experimental import pallas as pl
from jax.experimental.pallas import tpu as pltpu
from jax.sharding import PartitionSpec as P

HALO = 8
PAD = 6
TSPAN = 64
TAPS = 2 * PAD + 1
LANES = 128
NEAR = 8
OVER = 3 * NEAR
BAND = 2 * LANES
TALL = BAND + 2 * HALO
MESH = pl.DeviceIdType.MESH
F32 = jnp.float32
BF16 = jnp.bfloat16


def split(x):
    high = x.astype(BF16)
    return high, (x - high.astype(F32)).astype(BF16)


def iota(shape, axis):
    return lax.broadcasted_iota(jnp.int32, shape, axis)


def kernel(
    sizes,
    flux_hbm, inv_hbm, mask_hbm, psf_columns_hbm, psf_rows_hbm, times_hbm, rates_hbm,
    out,
    psf_columns, psf_rows, times, rates,
    flux, inv, mask, toeplitz, padded, shifted,
    pair_out_over, pair_out_mid, pair_in_over, pair_in_mid,
    own_over, own_mid, far_in_over, far_in_mid,
    up_out, down_out, up_in, down_in,
    small_sem, load_sem, pair_send, pair_recv, far_send, far_recv, row_send, row_recv,
):
    groups, row_devices = sizes
    epochs, rows, columns = flux.shape
    tiles = columns // LANES
    depth = epochs * rows
    me = lax.axis_index("epoch")
    core, group = lax.rem(me, 2), me // 2
    partner = me + 1 - 2 * core
    row = lax.axis_index("row")

    smalls = []
    for n, (src, dst) in enumerate((
        (psf_columns_hbm, psf_columns), (psf_rows_hbm, psf_rows), (times_hbm, times), (rates_hbm, rates),
    )):
        copy = pltpu.make_async_copy(src, dst, small_sem.at[n])
        copy.start()
        smalls.append(copy)
    loads = []
    for e in range(epochs):
        for n, (src, dst) in enumerate(((inv_hbm, inv), (mask_hbm, mask), (flux_hbm, flux))):
            copy = pltpu.make_async_copy(src.at[e], dst.at[e], load_sem.at[e, n])
            copy.start()
            loads.append(copy)

    barrier = pltpu.get_barrier_semaphore()
    pl.semaphore_signal(barrier, inc=1, device_id={"epoch": partner}, device_id_type=MESH)
    for d in range(1, groups):
        there = 2 * lax.rem(group + d, groups) + core
        pl.semaphore_signal(barrier, inc=1, device_id={"epoch": there}, device_id_type=MESH)

    @pl.when(row > 0)
    def _():
        pl.semaphore_signal(barrier, inc=1, device_id={"row": row - 1}, device_id_type=MESH)

    @pl.when(row < row_devices - 1)
    def _():
        pl.semaphore_signal(barrier, inc=1, device_id={"row": row + 1}, device_id_type=MESH)

    for copy in smalls:
        copy.wait()
    offset = BAND // 4 - PAD + HALO
    lane = iota((NEAR, LANES), 1)
    place = iota((NEAR, LANES), 0) - lane
    wrapped = lax.rem(place - offset + 4 * LANES, LANES)
    for e in range(epochs):
        plain = jnp.zeros((NEAR, LANES), F32)
        for tap in range(TAPS):
            plain = jnp.where(wrapped == tap, psf_columns[e, tap], plain)
        for m in range(TALL // NEAR):
            turned = pltpu.roll(plain, (NEAR * m) % LANES, 1) if (NEAR * m) % LANES else plain
            where = place + (NEAR * m - offset)
            turned = jnp.where((where >= 0) & (where < TAPS), turned, 0.0)
            toeplitz[e, 0, m * NEAR : (m + 1) * NEAR, :] = turned
            toeplitz[e, 1, m * NEAR : (m + 1) * NEAR, :] = turned * turned

    half_lane = iota((rows, LANES), 1) < LANES // 2
    for e in range(epochs):
        for copy in loads[3 * e : 3 * e + 3]:
            copy.wait()
        weights = inv[e] * mask[e].astype(F32)
        for f, field in enumerate((flux[e] * weights, weights)):
            turned = pltpu.roll(field, LANES // 2, 1)
            first = turned[:, :LANES]
            for n, piece in enumerate(split(turned)):
                padded[e, f, n, :, LANES:columns] = piece[:, LANES:]
            for n, piece in enumerate(split(jnp.where(half_lane, 0.0, first))):
                padded[e, f, n, :, :LANES] = piece
            for n, piece in enumerate(split(jnp.where(half_lane, first, 0.0))):
                padded[e, f, n, :, columns:] = piece

    def shift(v, axis, e):
        return (rates[axis, v] * times[e]) >> (TSPAN.bit_length() - 1)

    def row_matrices(v):
        shape = (OVER + rows + NEAR, depth)
        o, k = iota(shape, 0), iota(shape, 1)
        far = jnp.where(rates[0, v] >= 0, -2 * NEAR, rows + NEAR)
        r = jnp.where(o < NEAR, o - NEAR, rows + o - NEAR)
        r = jnp.where(o >= 2 * NEAR, o - 2 * NEAR + far, r)
        r = jnp.where(o >= OVER, o - OVER, r)
        epoch_of = k // rows
        step = jnp.zeros(shape, jnp.int32)
        for e in range(epochs):
            step = jnp.where(epoch_of == e, shift(v, 0, e), step)
        at = r + step
        good = (at + row * rows >= 0) & (at + row * rows < rows * row_devices) & (o < OVER + rows)
        tap_at = jnp.where(good, lax.rem(k, rows) - at + PAD, -1)
        one_row = epoch_of[:1]
        plain = jnp.zeros(shape, F32)
        for tap in range(TAPS):
            value = jnp.zeros((1, depth), F32)
            for e in range(epochs):
                value = jnp.where(one_row == e, psf_rows[e, tap], value)
            plain = jnp.where(tap_at == tap, value, plain)
        return split(plain), split(plain * plain)

    def columns_stage(pair, f):
        lanes = iota((rows, 2 * LANES), 1)
        for e in range(epochs):
            steps = [shift(v, 1, e) for v in pair]
            band = jnp.concatenate(
                [toeplitz[e, f, pl.ds(HALO - s, BAND), :] for s in steps], axis=1
            )
            band_high, band_low = split(band)
            high, low = (
                jnp.concatenate(
                    [padded[e, f, n, :, t * LANES : t * LANES + BAND] for t in range(tiles)], axis=0
                )
                for n in range(2)
            )
            result = jnp.dot(
                jnp.concatenate([high, low, high], axis=1),
                jnp.concatenate([band_high, band_high, band_low], axis=0),
                preferred_element_type=F32,
            )
            source = lax.rem(lanes, LANES) + jnp.where(lanes < LANES, steps[0], steps[1])
            for t in range(tiles):
                block = result[t * rows : (t + 1) * rows]
                if t == 0:
                    block = jnp.where(source >= 0, block, 0.0)
                if t == tiles - 1:
                    block = jnp.where(source + t * LANES < columns, block, 0.0)
                high_block, low_block = split(block)
                for h in range(2):
                    at = slice(t * LANES, (t + 1) * LANES)
                    part = slice(h * LANES, (h + 1) * LANES)
                    shifted[h, e * rows : (e + 1) * rows, at] = high_block[:, part]
                    shifted[h, depth + e * rows : depth + (e + 1) * rows, at] = low_block[:, part]

    def rows_stage(h, matrix):
        high, low = matrix
        return jnp.dot(
            jnp.concatenate([high, high], axis=1), shifted[h], preferred_element_type=F32
        ) + jnp.dot(low, shifted[h, :depth], preferred_element_type=F32)

    def pair_copy(d, f, part):
        src, dst = ((pair_out_over, pair_in_over), (pair_out_mid, pair_in_mid))[part]
        return pltpu.make_async_remote_copy(
            src_ref=src.at[d, f], dst_ref=dst.at[d, f],
            send_sem=pair_send.at[d, f, part], recv_sem=pair_recv.at[d, f, part],
            device_id={"epoch": partner}, device_id_type=MESH,
        )

    def far_copy(d, f, part):
        src, dst = ((own_over, far_in_over), (own_mid, far_in_mid))[part]
        return pltpu.make_async_remote_copy(
            src_ref=src.at[d, f], dst_ref=dst.at[d - 1, f],
            send_sem=far_send.at[d - 1, f, part], recv_sem=far_recv.at[d - 1, f, part],
            device_id={"epoch": 2 * lax.rem(group + d, groups) + core}, device_id_type=MESH,
        )

    def row_copy(f, way, other):
        src, dst = ((up_out, down_in), (down_out, up_in))[way]
        return pltpu.make_async_remote_copy(
            src_ref=src.at[f], dst_ref=dst.at[f],
            send_sem=row_send.at[f, way], recv_sem=row_recv.at[f, way],
            device_id={"row": other}, device_id_type=MESH,
        )

    def finish(d, f, part):
        own, arrived = ((own_over, pair_in_over), (own_mid, pair_in_mid))[part]
        pair_copy(d, f, part).wait_recv()
        own[d, f] = own[d, f] + arrived[d, f]
        if d:
            far_copy(d, f, part).start()

    order = list(range(1, groups)) + [0]
    waiting = []
    entered = False
    for d in order:
        goal = 2 * lax.rem(group + d, groups)
        pair = (goal + 1 - core, goal + core)
        matrices = [row_matrices(v) for v in pair]
        for f in range(2):
            columns_stage(pair, f)
            if not entered:
                above = lax.div(row + row_devices - 1, row_devices)
                below = lax.div(2 * row_devices - 2 - row, row_devices)
                pl.semaphore_wait(barrier, groups + above + below)
                entered = True
            for n in waiting:
                finish(*n)
            part = rows_stage(0, matrices[0][f])
            pair_out_over[d, f] = part[:OVER]
            pair_copy(d, f, 0).start()
            pair_out_mid[d, f] = part[OVER : OVER + rows]
            pair_copy(d, f, 1).start()
            part = rows_stage(1, matrices[1][f])
            own_over[d, f] = part[:OVER]
            own_mid[d, f] = part[OVER : OVER + rows]
            waiting = [(d, f, 0)] if f == 0 else [(d, 1, 0), (d, 0, 1), (d, 1, 1)]
    for n in waiting[:1]:
        finish(*n)

    upward = rates[0, me] >= 0
    for f in range(2):
        total = own_over[0, f]
        for d in range(1, groups):
            far_copy(d, f, 0).wait_recv()
            total = total + far_in_over[d - 1, f]
        far = total[2 * NEAR :]
        up_out[f, :NEAR] = jnp.where(upward, far, 0.0)
        up_out[f, NEAR:] = total[:NEAR]
        down_out[f, :NEAR] = total[NEAR : 2 * NEAR]
        down_out[f, NEAR:] = jnp.where(upward, 0.0, far)

        @pl.when(row > 0)
        def _():
            row_copy(f, 0, row - 1).start()

        @pl.when(row < row_devices - 1)
        def _():
            row_copy(f, 1, row + 1).start()

    for f in range(2):
        finish(0, f, 1)
        total = own_mid[0, f]
        for d in range(1, groups):
            far_copy(d, f, 1).wait_recv()
            total = total + far_in_mid[d - 1, f]
        out[f] = total

    for f in range(2):
        @pl.when(row > 0)
        def _():
            row_copy(f, 1, row - 1).wait_recv()
            out[f, : 2 * NEAR] = out[f, : 2 * NEAR] + up_in[f]

        @pl.when(row < row_devices - 1)
        def _():
            row_copy(f, 0, row + 1).wait_recv()
            out[f, rows - 2 * NEAR :] = out[f, rows - 2 * NEAR :] + down_in[f]

    for f in range(2):
        for part in range(2):
            for d in range(groups):
                pair_copy(d, f, part).wait_send()
            for d in range(1, groups):
                far_copy(d, f, part).wait_send()

        @pl.when(row > 0)
        def _():
            row_copy(f, 0, row - 1).wait_send()

        @pl.when(row < row_devices - 1)
        def _():
            row_copy(f, 1, row + 1).wait_send()


def solution(mesh):
    epoch_devices, row_devices = mesh.shape["epoch"], mesh.shape["row"]
    groups = epoch_devices // 2

    def on_device(flux_image, inv_var, pixel_mask, psf_columns, psf_rows, epoch_times, trial_rates):
        epochs, rows, columns = flux_image.shape
        depth = epochs * rows
        assert epoch_devices % 2 == 0 and trial_rates.shape[0] == epoch_devices
        assert rows % (2 * NEAR) == 0 and columns % LANES == 0 and depth % LANES == 0
        far = max(groups - 1, 1)
        hbm = pl.BlockSpec(memory_space=pl.ANY)
        vmem = pl.BlockSpec(memory_space=pltpu.VMEM)
        image = (epochs, rows, columns)

        def pieces(count):
            return [
                pltpu.VMEM((count, 2, OVER, columns), F32),
                pltpu.VMEM((count, 2, rows, columns), F32),
            ]

        edge = pltpu.VMEM((2, 2 * NEAR, columns), F32)
        dma = pltpu.SemaphoreType.DMA
        stacks = pl.pallas_call(
            functools.partial(kernel, (groups, row_devices)),
            out_shape=pltpu.VMEM((2, rows, columns), F32),
            in_specs=[hbm] * 7,
            out_specs=vmem,
            scratch_shapes=[
                pltpu.SMEM(psf_columns.shape, F32),
                pltpu.SMEM(psf_rows.shape, F32),
                pltpu.SMEM(epoch_times.shape, jnp.int32),
                pltpu.SMEM(trial_rates.shape[::-1], jnp.int32),
                pltpu.VMEM(image, F32),
                pltpu.VMEM(image, F32),
                pltpu.VMEM(image, jnp.int32),
                pltpu.VMEM((epochs, 2, TALL, LANES), F32),
                pltpu.VMEM((epochs, 2, 2, rows, columns + LANES), BF16),
                pltpu.VMEM((2, 2 * depth, columns), BF16),
                *pieces(groups),
                *pieces(groups),
                *pieces(groups),
                *pieces(far),
                edge, edge, edge, edge,
                dma((4,)),
                dma((epochs, 3)),
                dma((groups, 2, 2)),
                dma((groups, 2, 2)),
                dma((far, 2, 2)),
                dma((far, 2, 2)),
                dma((2, 2)),
                dma((2, 2)),
            ],
            compiler_params=pltpu.CompilerParams(collective_id=0, has_side_effects=True),
        )(flux_image, inv_var, pixel_mask, psf_columns, psf_rows, epoch_times, trial_rates.T)
        return stacks[:1], stacks[1:]

    in_specs = (
        P("epoch", "row", None),
        P("epoch", "row", None),
        P("epoch", "row", None),
        P("epoch", None),
        P("epoch", None),
        P("epoch"),
        P(),
    )
    out_specs = (P("epoch", "row", None), P("epoch", "row", None))
    return jax.shard_map(
        on_device, mesh=mesh, in_specs=in_specs, out_specs=out_specs, check_vma=False
    )
```

```python
import functools

import jax
import jax.numpy as jnp
from jax import lax
from jax.experimental import pallas as pl
from jax.experimental.pallas import tpu as pltpu
from jax.sharding import PartitionSpec as P

HALO = 8
PAD = 6
TSPAN = 64
TAPS = 2 * PAD + 1
LANES = 128
NEAR = 8
OVER = 3 * NEAR
EDGES = 2 * NEAR
BAND = 2 * LANES
TALL = BAND + 2 * HALO
MESH = pl.DeviceIdType.MESH
F32 = jnp.float32
BF16 = jnp.bfloat16


def split(x):
    high = x.astype(BF16)
    return high, (x - high.astype(F32)).astype(BF16)


def iota(shape, axis):
    return lax.broadcasted_iota(jnp.int32, shape, axis)


def kernel(
    sizes,
    flux_hbm, inv_hbm, mask_hbm, psf_columns_hbm, psf_rows_hbm, times_hbm, rates_hbm,
    out,
    psf_columns, psf_rows, times, rates,
    flux, inv, mask, toeplitz, padded, shifted,
    pair_out_over, pair_out_mid, pair_in_over, pair_in_mid,
    own_over, own_mid, far_out, far_in_over, far_in_mid,
    near_out, near_in, row_out, row_in,
    small_sem, load_sem, pair_send, pair_recv, far_send, far_recv,
    near_send, near_recv, row_send, row_recv,
):
    groups, row_devices = sizes
    epochs, rows, columns = flux.shape
    tiles = columns // LANES
    depth = epochs * rows
    center = rows - EDGES
    me = lax.axis_index("epoch")
    core, group = lax.rem(me, 2), me // 2
    partner = me + 1 - 2 * core
    row = lax.axis_index("row")

    smalls = []
    for n, (src, dst) in enumerate((
        (psf_columns_hbm, psf_columns), (psf_rows_hbm, psf_rows), (times_hbm, times), (rates_hbm, rates),
    )):
        copy = pltpu.make_async_copy(src, dst, small_sem.at[n])
        copy.start()
        smalls.append(copy)
    loads = []
    for e in range(epochs):
        for n, (src, dst) in enumerate(((inv_hbm, inv), (mask_hbm, mask), (flux_hbm, flux))):
            copy = pltpu.make_async_copy(src.at[e], dst.at[e], load_sem.at[e, n])
            copy.start()
            loads.append(copy)

    barrier = pltpu.get_barrier_semaphore()
    pl.semaphore_signal(barrier, inc=1, device_id={"epoch": partner}, device_id_type=MESH)
    for d in range(1, groups):
        there = 2 * lax.rem(group + d, groups) + core
        pl.semaphore_signal(barrier, inc=1, device_id={"epoch": there}, device_id_type=MESH)

    @pl.when(row > 0)
    def _():
        pl.semaphore_signal(barrier, inc=1, device_id={"row": row - 1}, device_id_type=MESH)

    @pl.when(row < row_devices - 1)
    def _():
        pl.semaphore_signal(barrier, inc=1, device_id={"row": row + 1}, device_id_type=MESH)

    for copy in smalls:
        copy.wait()
    offset = BAND // 4 - PAD + HALO
    lane = iota((NEAR, LANES), 1)
    place = iota((NEAR, LANES), 0) - lane
    wrapped = lax.rem(place - offset + 4 * LANES, LANES)
    for e in range(epochs):
        plain = jnp.zeros((NEAR, LANES), F32)
        for tap in range(TAPS):
            plain = jnp.where(wrapped == tap, psf_columns[e, tap], plain)
        for m in range(TALL // NEAR):
            turned = pltpu.roll(plain, (NEAR * m) % LANES, 1) if (NEAR * m) % LANES else plain
            where = place + (NEAR * m - offset)
            turned = jnp.where((where >= 0) & (where < TAPS), turned, 0.0)
            toeplitz[e, 0, m * NEAR : (m + 1) * NEAR, :] = turned
            toeplitz[e, 1, m * NEAR : (m + 1) * NEAR, :] = turned * turned

    half_lane = iota((rows, LANES), 1) < LANES // 2
    for e in range(epochs):
        for copy in loads[3 * e : 3 * e + 3]:
            copy.wait()
        weights = inv[e] * mask[e].astype(F32)
        for f, field in enumerate((flux[e] * weights, weights)):
            turned = pltpu.roll(field, LANES // 2, 1)
            first = turned[:, :LANES]
            for n, piece in enumerate(split(turned)):
                padded[e, f, n, :, LANES:columns] = piece[:, LANES:]
            for n, piece in enumerate(split(jnp.where(half_lane, 0.0, first))):
                padded[e, f, n, :, :LANES] = piece
            for n, piece in enumerate(split(jnp.where(half_lane, first, 0.0))):
                padded[e, f, n, :, columns:] = piece

    def shift(v, axis, e):
        return (rates[axis, v] * times[e]) >> (TSPAN.bit_length() - 1)

    def row_matrices(v):
        shape = (OVER + rows + NEAR, depth)
        o, k = iota(shape, 0), iota(shape, 1)
        far = jnp.where(rates[0, v] >= 0, -PAD - NEAR, rows + PAD)
        r = jnp.where(o < NEAR, o + far, o - NEAR - PAD)
        r = jnp.where(o >= 2 * NEAR, o - 2 * NEAR + rows, r)
        r = jnp.where(o >= OVER, o - OVER + NEAR, r)
        r = jnp.where(o >= OVER + center, o - OVER - center, r)
        r = jnp.where(o >= OVER + rows - NEAR, o - OVER, r)
        spare = (o >= OVER + rows) | ((o >= NEAR + PAD) & (o < 2 * NEAR))
        spare = spare | ((o >= 2 * NEAR + PAD) & (o < OVER))
        epoch_of = k // rows
        step = jnp.zeros(shape, jnp.int32)
        for e in range(epochs):
            step = jnp.where(epoch_of == e, shift(v, 0, e), step)
        at = r + step
        good = (at + row * rows >= 0) & (at + row * rows < rows * row_devices) & ~spare
        tap_at = jnp.where(good, lax.rem(k, rows) - at + PAD, -1)
        one_row = epoch_of[:1]
        plain = jnp.zeros(shape, F32)
        for tap in range(TAPS):
            value = jnp.zeros((1, depth), F32)
            for e in range(epochs):
                value = jnp.where(one_row == e, psf_rows[e, tap], value)
            plain = jnp.where(tap_at == tap, value, plain)
        return split(plain), split(plain * plain)

    def columns_stage(pair, f):
        lanes = iota((rows, 2 * LANES), 1)
        for e in range(epochs):
            steps = [shift(v, 1, e) for v in pair]
            band = jnp.concatenate(
                [toeplitz[e, f, pl.ds(HALO - s, BAND), :] for s in steps], axis=1
            )
            band_high, band_low = split(band)
            high, low = (
                jnp.concatenate(
                    [padded[e, f, n, :, t * LANES : t * LANES + BAND] for t in range(tiles)], axis=0
                )
                for n in range(2)
            )
            result = jnp.dot(
                jnp.concatenate([high, low, high], axis=1),
                jnp.concatenate([band_high, band_high, band_low], axis=0),
                preferred_element_type=F32,
            )
            source = lax.rem(lanes, LANES) + jnp.where(lanes < LANES, steps[0], steps[1])
            for t in range(tiles):
                block = result[t * rows : (t + 1) * rows]
                if t == 0:
                    block = jnp.where(source >= 0, block, 0.0)
                if t == tiles - 1:
                    block = jnp.where(source + t * LANES < columns, block, 0.0)
                high_block, low_block = split(block)
                for h in range(2):
                    at = slice(t * LANES, (t + 1) * LANES)
                    part = slice(h * LANES, (h + 1) * LANES)
                    shifted[h, e * rows : (e + 1) * rows, at] = high_block[:, part]
                    shifted[h, depth + e * rows : depth + (e + 1) * rows, at] = low_block[:, part]

    def rows_stage(h, matrix):
        high, low = matrix
        return jnp.dot(
            jnp.concatenate([high, high], axis=1), shifted[h], preferred_element_type=F32
        ) + jnp.dot(low, shifted[h, :depth], preferred_element_type=F32)

    def pair_copy(d, f, part):
        src, dst = ((pair_out_over, pair_in_over), (pair_out_mid, pair_in_mid))[part]
        return pltpu.make_async_remote_copy(
            src_ref=src.at[d, f], dst_ref=dst.at[d, f],
            send_sem=pair_send.at[d, f, part], recv_sem=pair_recv.at[d, f, part],
            device_id={"epoch": partner}, device_id_type=MESH,
        )

    def far_copy(d, f, part):
        src, dst = (
            (far_out.at[d - 1, f], far_in_over.at[d - 1, f]),
            (own_mid.at[d, f, :center], far_in_mid.at[d - 1, f, :center]),
            (own_mid.at[d, f, center:], far_in_mid.at[d - 1, f, center:]),
        )[part]
        return pltpu.make_async_remote_copy(
            src_ref=src, dst_ref=dst,
            send_sem=far_send.at[d - 1, f, part], recv_sem=far_recv.at[d - 1, f, part],
            device_id={"epoch": 2 * lax.rem(group + d, groups) + core}, device_id_type=MESH,
        )

    neighbours = ((row > 0, row - 1), (row < row_devices - 1, row + 1))

    def near_copy(d, f, way):
        return pltpu.make_async_remote_copy(
            src_ref=near_out.at[d, f, way], dst_ref=near_in.at[d, f, way],
            send_sem=near_send.at[d, f, way], recv_sem=near_recv.at[d, f, way],
            device_id={"row": neighbours[way][1]}, device_id_type=MESH,
        )

    def row_copy(f, way):
        return pltpu.make_async_remote_copy(
            src_ref=row_out.at[f, way], dst_ref=row_in.at[f, way],
            send_sem=row_send.at[f, way], recv_sem=row_recv.at[f, way],
            device_id={"row": neighbours[way][1]}, device_id_type=MESH,
        )

    def to_neighbours(copy_of, *which):
        for way in range(2):
            @pl.when(neighbours[way][0])
            def _():
                copy_of(*which, way).start()

    def from_neighbours(copy_of, which, add):
        for way in range(2):
            @pl.when(neighbours[1 - way][0])
            def _():
                copy_of(*which, way).wait_recv()
                add(way)

    def finish_over(d, f):
        pair_copy(d, f, 0).wait_recv()
        total = own_over[d, f] + pair_in_over[d, f]
        if d:
            far_out[d - 1, f] = total[:NEAR]
            far_copy(d, f, 0).start()
        else:
            own_over[0, f, :NEAR] = total[:NEAR]
        for way in range(2):
            near_out[d, f, way] = total[(way + 1) * NEAR : (way + 1) * NEAR + PAD]
        to_neighbours(near_copy, d, f)

    def finish_mid(d, f):
        pair_copy(d, f, 1).wait_recv()
        own_mid[d, f] = own_mid[d, f] + pair_in_mid[d, f]
        far_copy(d, f, 1).start()

    def finish_edges(d, f):
        def add(way):
            at = slice(rows - PAD, rows) if way == 0 else slice(center, center + PAD)
            own_mid[d, f, at] = own_mid[d, f, at] + near_in[d, f, way]

        from_neighbours(near_copy, (d, f), add)
        far_copy(d, f, 2).start()

    items = [(d, f) for d in (*range(1, groups), 0) for f in range(2)]
    edges_left = [item for item in items if item[0]]
    for n, (d, f) in enumerate(items):
        goal = 2 * lax.rem(group + d, groups)
        pair = (goal + 1 - core, goal + core)
        if f == 0:
            matrices = [row_matrices(v) for v in pair]
        columns_stage(pair, f)
        if n == 0:
            above = lax.div(row + row_devices - 1, row_devices)
            below = lax.div(2 * row_devices - 2 - row, row_devices)
            pl.semaphore_wait(barrier, groups + above + below)
        else:
            before = items[n - 1]
            finish_over(*before)
            if before[0]:
                finish_mid(*before)
        if n >= 3 and edges_left:
            finish_edges(*edges_left.pop(0))
        part = rows_stage(0, matrices[0][f])
        pair_out_over[d, f] = part[:OVER]
        pair_copy(d, f, 0).start()
        pair_out_mid[d, f] = part[OVER : OVER + rows]
        pair_copy(d, f, 1).start()
        part = rows_stage(1, matrices[1][f])
        own_over[d, f] = part[:OVER]
        own_mid[d, f] = part[OVER : OVER + rows]
    for item in edges_left:
        finish_edges(*item)
    finish_over(*items[-1])

    upward = rates[0, me] >= 0
    for f in range(2):
        far = own_over[0, f, :NEAR]
        for d in range(1, groups):
            far_copy(d, f, 0).wait_recv()
            far = far + far_in_over[d - 1, f]
        row_out[f, 0] = jnp.where(upward, far, 0.0)
        row_out[f, 1] = jnp.where(upward, 0.0, far)
        to_neighbours(row_copy, f)

    def add_to(f, at, value):
        out[f, at] = out[f, at] + value

    for f in range(2):
        pair_copy(0, f, 1).wait_recv()
        total = own_mid[0, f] + pair_in_mid[0, f]
        out[f, NEAR : rows - NEAR] = total[:center]
        out[f, :NEAR] = total[center : center + NEAR]
        out[f, rows - NEAR :] = total[center + NEAR :]
        from_neighbours(near_copy, (0, f), lambda way: add_to(
            f, slice(rows - PAD, rows) if way == 0 else slice(0, PAD), near_in[0, f, way]
        ))
    for f in range(2):
        for d in range(1, groups):
            far_copy(d, f, 1).wait_recv()
            add_to(f, slice(NEAR, rows - NEAR), far_in_mid[d - 1, f, :center])
    for f in range(2):
        from_neighbours(row_copy, (f,), lambda way: add_to(
            f, slice(rows - PAD - NEAR, rows - PAD) if way == 0 else slice(PAD, PAD + NEAR), row_in[f, way]
        ))
        for d in range(1, groups):
            far_copy(d, f, 2).wait_recv()
            add_to(f, slice(0, NEAR), far_in_mid[d - 1, f, center : center + NEAR])
            add_to(f, slice(rows - NEAR, rows), far_in_mid[d - 1, f, center + NEAR :])

    for f in range(2):
        for d in range(groups):
            for part in range(2):
                pair_copy(d, f, part).wait_send()
        for d in range(1, groups):
            for part in range(3):
                far_copy(d, f, part).wait_send()
        for way in range(2):
            @pl.when(neighbours[way][0])
            def _():
                for d in range(groups):
                    near_copy(d, f, way).wait_send()
                row_copy(f, way).wait_send()


def solution(mesh):
    epoch_devices, row_devices = mesh.shape["epoch"], mesh.shape["row"]
    groups = epoch_devices // 2

    def on_device(flux_image, inv_var, pixel_mask, psf_columns, psf_rows, epoch_times, trial_rates):
        epochs, rows, columns = flux_image.shape
        depth = epochs * rows
        assert epoch_devices % 2 == 0 and trial_rates.shape[0] == epoch_devices
        assert rows % (2 * NEAR) == 0 and rows > 2 * NEAR and columns % LANES == 0 and depth % LANES == 0
        far = max(groups - 1, 1)
        hbm = pl.BlockSpec(memory_space=pl.ANY)
        vmem = pl.BlockSpec(memory_space=pltpu.VMEM)
        image = (epochs, rows, columns)

        def pieces(count):
            return [
                pltpu.VMEM((count, 2, OVER, columns), F32),
                pltpu.VMEM((count, 2, rows, columns), F32),
            ]

        def edge(*size):
            return pltpu.VMEM((*size, columns), F32)

        dma = pltpu.SemaphoreType.DMA
        stacks = pl.pallas_call(
            functools.partial(kernel, (groups, row_devices)),
            out_shape=pltpu.VMEM((2, rows, columns), F32),
            in_specs=[hbm] * 7,
            out_specs=vmem,
            scratch_shapes=[
                pltpu.SMEM(psf_columns.shape, F32),
                pltpu.SMEM(psf_rows.shape, F32),
                pltpu.SMEM(epoch_times.shape, jnp.int32),
                pltpu.SMEM(trial_rates.shape[::-1], jnp.int32),
                pltpu.VMEM(image, F32),
                pltpu.VMEM(image, F32),
                pltpu.VMEM(image, jnp.int32),
                pltpu.VMEM((epochs, 2, TALL, LANES), F32),
                pltpu.VMEM((epochs, 2, 2, rows, columns + LANES), BF16),
                pltpu.VMEM((2, 2 * depth, columns), BF16),
                *pieces(groups),
                *pieces(groups),
                *pieces(groups),
                edge(far, 2, NEAR),
                edge(far, 2, NEAR),
                edge(far, 2, rows),
                edge(groups, 2, 2, PAD),
                edge(groups, 2, 2, PAD),
                edge(2, 2, NEAR),
                edge(2, 2, NEAR),
                dma((4,)),
                dma((epochs, 3)),
                dma((groups, 2, 2)),
                dma((groups, 2, 2)),
                dma((far, 2, 3)),
                dma((far, 2, 3)),
                dma((groups, 2, 2)),
                dma((groups, 2, 2)),
                dma((2, 2)),
                dma((2, 2)),
            ],
            compiler_params=pltpu.CompilerParams(collective_id=0, has_side_effects=True),
        )(flux_image, inv_var, pixel_mask, psf_columns, psf_rows, epoch_times, trial_rates.T)
        return stacks[:1], stacks[1:]

    in_specs = (
        P("epoch", "row", None),
        P("epoch", "row", None),
        P("epoch", "row", None),
        P("epoch", None),
        P("epoch", None),
        P("epoch"),
        P(),
    )
    out_specs = (P("epoch", "row", None), P("epoch", "row", None))
    return jax.shard_map(
        on_device, mesh=mesh, in_specs=in_specs, out_specs=out_specs, check_vma=False
    )
```

```python
import functools

import jax
import jax.numpy as jnp
from jax import lax
from jax.experimental import pallas as pl
from jax.experimental.pallas import tpu as pltpu
from jax.sharding import PartitionSpec as P

HALO = 8
PAD = 6
TSPAN = 64
TAPS = 2 * PAD + 1
LANES = 128
NEAR = 8
OVER = 3 * NEAR
EDGES = 2 * NEAR
BAND = 2 * LANES
FIELDS = (1, 0)
MESH = pl.DeviceIdType.MESH
F32 = jnp.float32
BF16 = jnp.bfloat16


def split(x):
    high = x.astype(BF16)
    return high, (x - high.astype(F32)).astype(BF16)


def iota(shape, axis):
    return lax.broadcasted_iota(jnp.int32, shape, axis)


def kernel(
    sizes,
    flux_hbm, inv_hbm, mask_hbm, psf_columns_hbm, psf_rows_hbm, times_hbm, rates_hbm,
    out,
    psf_columns, psf_rows, times, rates,
    flux, inv, mask, toeplitz, padded, convolved, shifted,
    pair_out_over, pair_out_mid, pair_in_over, pair_in_mid,
    own_over, own_mid, far_out, far_in_over, far_in_mid,
    near_out, near_in, row_out, row_in,
    small_sem, load_sem, pair_send, pair_recv, far_send, far_recv,
    near_send, near_recv, row_send, row_recv,
):
    groups, row_devices = sizes
    epochs, rows, columns = flux.shape
    tiles = columns // LANES
    depth = epochs * rows
    center = rows - EDGES
    me = lax.axis_index("epoch")
    core, group = lax.rem(me, 2), me // 2
    partner = me + 1 - 2 * core
    row = lax.axis_index("row")

    smalls = []
    for n, (src, dst) in enumerate((
        (psf_columns_hbm, psf_columns), (psf_rows_hbm, psf_rows), (times_hbm, times), (rates_hbm, rates),
    )):
        copy = pltpu.make_async_copy(src, dst, small_sem.at[n])
        copy.start()
        smalls.append(copy)
    loads = []
    for n, (src, dst) in enumerate(((inv_hbm, inv), (mask_hbm, mask), (flux_hbm, flux))):
        copies = [pltpu.make_async_copy(src.at[e], dst.at[e], load_sem.at[e, n]) for e in range(epochs)]
        loads.append(copies)
    for e in range(epochs):
        loads[0][e].start()
        loads[1][e].start()
    for e in range(epochs):
        loads[2][e].start()

    barrier = pltpu.get_barrier_semaphore()
    pl.semaphore_signal(barrier, inc=1, device_id={"epoch": partner}, device_id_type=MESH)
    for d in range(1, groups):
        there = 2 * lax.rem(group + d, groups) + core
        pl.semaphore_signal(barrier, inc=1, device_id={"epoch": there}, device_id_type=MESH)

    @pl.when(row > 0)
    def _():
        pl.semaphore_signal(barrier, inc=1, device_id={"row": row - 1}, device_id_type=MESH)

    @pl.when(row < row_devices - 1)
    def _():
        pl.semaphore_signal(barrier, inc=1, device_id={"row": row + 1}, device_id_type=MESH)

    for copy in smalls:
        copy.wait()
    offset = BAND // 4 - PAD - HALO
    tall = 2 * NEAR
    place = iota((tall, LANES), 0) - iota((tall, LANES), 1)
    wrapped = lax.rem(place - offset + 4 * LANES, LANES)
    for e in range(epochs):
        plain = jnp.zeros((tall, LANES), F32)
        for tap in range(TAPS):
            plain = jnp.where(wrapped == tap, psf_columns[e, tap], plain)
        for m in range(BAND // tall):
            turned = pltpu.roll(plain, (tall * m) % LANES, 1) if (tall * m) % LANES else plain
            where = place + (tall * m - offset)
            turned = jnp.where((where >= 0) & (where < TAPS), turned, 0.0)
            for f, value in enumerate((turned, turned * turned)):
                for n, piece in enumerate(split(value)):
                    toeplitz[e, f, m * tall : (m + 1) * tall, n * LANES : (n + 1) * LANES] = piece

    def shift(v, axis, e):
        return (rates[axis, v] * times[e]) >> (TSPAN.bit_length() - 1)

    def row_matrices(v):
        shape = (OVER + rows + NEAR, depth)
        o, k = iota(shape, 0), iota(shape, 1)
        far = jnp.where(rates[0, v] >= 0, -PAD - NEAR, rows + PAD)
        r = jnp.where(o < NEAR, o + far, o - NEAR - PAD)
        r = jnp.where(o >= 2 * NEAR, o - 2 * NEAR + rows, r)
        r = jnp.where(o >= OVER, o - OVER + NEAR, r)
        r = jnp.where(o >= OVER + center, o - OVER - center, r)
        r = jnp.where(o >= OVER + rows - NEAR, o - OVER, r)
        spare = (o >= OVER + rows) | ((o >= NEAR + PAD) & (o < 2 * NEAR))
        spare = spare | ((o >= 2 * NEAR + PAD) & (o < OVER))
        epoch_of = k // rows
        step = jnp.zeros(shape, jnp.int32)
        for e in range(epochs):
            step = jnp.where(epoch_of == e, shift(v, 0, e), step)
        at = r + step
        good = (at + row * rows >= 0) & (at + row * rows < rows * row_devices) & ~spare
        tap_at = jnp.where(good, lax.rem(k, rows) - at + PAD, -1)
        one_row = epoch_of[:1]
        plain = jnp.zeros(shape, F32)
        for tap in range(TAPS):
            value = jnp.zeros((1, depth), F32)
            for e in range(epochs):
                value = jnp.where(one_row == e, psf_rows[e, tap], value)
            plain = jnp.where(tap_at == tap, value, plain)
        stacks = []
        for value in (plain, plain * plain):
            high, low = split(value)
            both = jnp.concatenate([high, low], axis=0)
            stacks.append(jnp.concatenate([both, both], axis=1))
        return stacks

    half_lane = iota((rows, LANES), 1) < LANES // 2
    lane = iota((rows, LANES), 1)

    def prepare(e, f):
        if f == FIELDS[0]:
            loads[0][e].wait()
            loads[1][e].wait()
        if f == 0:
            loads[2][e].wait()
        field = inv[e] * mask[e].astype(F32)
        if f == 0:
            field = flux[e] * field
        turned = pltpu.roll(field, LANES // 2, 1)
        first = turned[:, :LANES]
        for n, piece in enumerate(split(turned)):
            padded[e, f, n, :, LANES:columns] = piece[:, LANES:]
        for n, piece in enumerate(split(jnp.where(half_lane, 0.0, first))):
            padded[e, f, n, :, :LANES] = piece
        for n, piece in enumerate(split(jnp.where(half_lane, first, 0.0))):
            padded[e, f, n, :, columns : columns + LANES] = piece
            padded[e, f, n, :, columns + LANES :] = jnp.zeros((rows, LANES), BF16)

    def convolve(e, f):
        windows = [
            padded[e, f, n, :, t * LANES : t * LANES + BAND] for n in range(2) for t in range(tiles + 1)
        ]
        result = jnp.dot(
            jnp.concatenate(windows, axis=0), toeplitz[e, f], preferred_element_type=F32
        )
        middle = (tiles + 1) * rows
        result = result[:middle, :LANES] + (result[:middle, LANES:] + result[middle:, :LANES])
        for t in range(tiles + 1):
            block = result[t * rows : (t + 1) * rows]
            if t == 0:
                block = jnp.where(lane >= HALO, block, 0.0)
            if t == tiles:
                block = jnp.where(lane < HALO, block, 0.0)
            for n, piece in enumerate(split(block)):
                at = slice(n * depth + e * rows, n * depth + (e + 1) * rows)
                convolved[f, at, t * LANES : (t + 1) * LANES] = piece

    def columns_stage(h, v, f):
        for e in range(epochs):
            step = shift(v, 1, e) + HALO
            stay = lane < LANES - step
            turn = lax.rem(LANES - step, LANES)
            for n in range(2):
                at = slice(n * depth + e * rows, n * depth + (e + 1) * rows)
                turned = [
                    pltpu.roll(convolved[f, at, t * LANES : (t + 1) * LANES], turn, 1)
                    for t in range(tiles + 1)
                ]
                for t in range(tiles):
                    shifted[h, at, t * LANES : (t + 1) * LANES] = jnp.where(stay, turned[t], turned[t + 1])

    def rows_stage(h, matrix):
        result = jnp.dot(matrix, shifted[h], preferred_element_type=F32)
        half = matrix.shape[0] // 2
        return result[:half] + result[half:]

    def pair_copy(d, f, part):
        src, dst = ((pair_out_over, pair_in_over), (pair_out_mid, pair_in_mid))[part]
        return pltpu.make_async_remote_copy(
            src_ref=src.at[d, f], dst_ref=dst.at[d, f],
            send_sem=pair_send.at[d, f, part], recv_sem=pair_recv.at[d, f, part],
            device_id={"epoch": partner}, device_id_type=MESH,
        )

    def far_copy(d, f, part):
        src, dst = (
            (far_out.at[d - 1, f], far_in_over.at[d - 1, f]),
            (own_mid.at[d, f, :center], far_in_mid.at[d - 1, f, :center]),
            (own_mid.at[d, f, center:], far_in_mid.at[d - 1, f, center:]),
        )[part]
        return pltpu.make_async_remote_copy(
            src_ref=src, dst_ref=dst,
            send_sem=far_send.at[d - 1, f, part], recv_sem=far_recv.at[d - 1, f, part],
            device_id={"epoch": 2 * lax.rem(group + d, groups) + core}, device_id_type=MESH,
        )

    neighbours = ((row > 0, row - 1), (row < row_devices - 1, row + 1))

    def near_copy(d, f, way):
        return pltpu.make_async_remote_copy(
            src_ref=near_out.at[d, f, way], dst_ref=near_in.at[d, f, way],
            send_sem=near_send.at[d, f, way], recv_sem=near_recv.at[d, f, way],
            device_id={"row": neighbours[way][1]}, device_id_type=MESH,
        )

    def row_copy(f, way):
        return pltpu.make_async_remote_copy(
            src_ref=row_out.at[f, way], dst_ref=row_in.at[f, way],
            send_sem=row_send.at[f, way], recv_sem=row_recv.at[f, way],
            device_id={"row": neighbours[way][1]}, device_id_type=MESH,
        )

    def to_neighbours(copy_of, *which):
        for way in range(2):
            @pl.when(neighbours[way][0])
            def _():
                copy_of(*which, way).start()

    def from_neighbours(copy_of, which, add):
        for way in range(2):
            @pl.when(neighbours[1 - way][0])
            def _():
                copy_of(*which, way).wait_recv()
                add(way)

    def finish_over(d, f):
        pair_copy(d, f, 0).wait_recv()
        total = own_over[d, f] + pair_in_over[d, f]
        if d:
            far_out[d - 1, f] = total[:NEAR]
            far_copy(d, f, 0).start()
        else:
            own_over[0, f, :NEAR] = total[:NEAR]
        for way in range(2):
            near_out[d, f, way] = total[(way + 1) * NEAR : (way + 1) * NEAR + PAD]
        to_neighbours(near_copy, d, f)

    def finish_mid(d, f):
        pair_copy(d, f, 1).wait_recv()
        own_mid[d, f] = own_mid[d, f] + pair_in_mid[d, f]
        far_copy(d, f, 1).start()

    def finish_edges(d, f):
        def add(way):
            at = slice(rows - PAD, rows) if way == 0 else slice(center, center + PAD)
            own_mid[d, f, at] = own_mid[d, f, at] + near_in[d, f, way]

        from_neighbours(near_copy, (d, f), add)
        far_copy(d, f, 2).start()

    def pair_of(d):
        goal = 2 * lax.rem(group + d, groups)
        return goal + 1 - core, goal + core

    order = (*range(1, groups), 0)
    items = [(d, f) for d in order for f in FIELDS]
    matrices = [row_matrices(v) for v in pair_of(order[0])]
    for n, (d, f) in enumerate(items):
        pair = pair_of(d)
        if n < 2:
            for e in range(epochs):
                prepare(e, f)
                convolve(e, f)
        elif f == FIELDS[0]:
            matrices = [row_matrices(v) for v in pair]
        columns_stage(0, pair[0], f)
        part = rows_stage(0, matrices[0][f])
        if n == 0:
            above = lax.div(row + row_devices - 1, row_devices)
            below = lax.div(2 * row_devices - 2 - row, row_devices)
            pl.semaphore_wait(barrier, groups + above + below)
        pair_out_over[d, f] = part[:OVER]
        pair_copy(d, f, 0).start()
        pair_out_mid[d, f] = part[OVER : OVER + rows]
        pair_copy(d, f, 1).start()
        columns_stage(1, pair[1], f)
        part = rows_stage(1, matrices[1][f])
        own_over[d, f] = part[:OVER]
        own_mid[d, f] = part[OVER : OVER + rows]
        if n:
            before = items[n - 1]
            finish_over(*before)
            if before[0]:
                finish_mid(*before)
    finish_over(*items[-1])
    for item in items:
        if item[0]:
            finish_edges(*item)

    upward = rates[0, me] >= 0
    for f in FIELDS:
        far = own_over[0, f, :NEAR]
        for d in range(1, groups):
            far_copy(d, f, 0).wait_recv()
            far = far + far_in_over[d - 1, f]
        row_out[f, 0] = jnp.where(upward, far, 0.0)
        row_out[f, 1] = jnp.where(upward, 0.0, far)
        to_neighbours(row_copy, f)

    def add_to(f, at, value):
        out[f, at] = out[f, at] + value

    for f in FIELDS:
        pair_copy(0, f, 1).wait_recv()
        total = own_mid[0, f] + pair_in_mid[0, f]
        out[f, NEAR : rows - NEAR] = total[:center]
        out[f, :NEAR] = total[center : center + NEAR]
        out[f, rows - NEAR :] = total[center + NEAR :]
        from_neighbours(near_copy, (0, f), lambda way: add_to(
            f, slice(rows - PAD, rows) if way == 0 else slice(0, PAD), near_in[0, f, way]
        ))
    for f in FIELDS:
        for d in range(1, groups):
            far_copy(d, f, 1).wait_recv()
            add_to(f, slice(NEAR, rows - NEAR), far_in_mid[d - 1, f, :center])
    for f in FIELDS:
        from_neighbours(row_copy, (f,), lambda way: add_to(
            f, slice(rows - PAD - NEAR, rows - PAD) if way == 0 else slice(PAD, PAD + NEAR), row_in[f, way]
        ))
        for d in range(1, groups):
            far_copy(d, f, 2).wait_recv()
            add_to(f, slice(0, NEAR), far_in_mid[d - 1, f, center : center + NEAR])
            add_to(f, slice(rows - NEAR, rows), far_in_mid[d - 1, f, center + NEAR :])

    for f in range(2):
        for d in range(groups):
            for part in range(2):
                pair_copy(d, f, part).wait_send()
        for d in range(1, groups):
            for part in range(3):
                far_copy(d, f, part).wait_send()
        for way in range(2):
            @pl.when(neighbours[way][0])
            def _():
                for d in range(groups):
                    near_copy(d, f, way).wait_send()
                row_copy(f, way).wait_send()


def solution(mesh):
    epoch_devices, row_devices = mesh.shape["epoch"], mesh.shape["row"]
    groups = epoch_devices // 2

    def on_device(flux_image, inv_var, pixel_mask, psf_columns, psf_rows, epoch_times, trial_rates):
        epochs, rows, columns = flux_image.shape
        depth = epochs * rows
        assert epoch_devices % 2 == 0 and trial_rates.shape[0] == epoch_devices
        assert rows % (2 * NEAR) == 0 and rows > 2 * NEAR and columns % LANES == 0 and depth % LANES == 0
        far = max(groups - 1, 1)
        hbm = pl.BlockSpec(memory_space=pl.ANY)
        vmem = pl.BlockSpec(memory_space=pltpu.VMEM)
        image = (epochs, rows, columns)

        def pieces(count):
            return [
                pltpu.VMEM((count, 2, OVER, columns), F32),
                pltpu.VMEM((count, 2, rows, columns), F32),
            ]

        def edge(*size):
            return pltpu.VMEM((*size, columns), F32)

        dma = pltpu.SemaphoreType.DMA
        stacks = pl.pallas_call(
            functools.partial(kernel, (groups, row_devices)),
            out_shape=pltpu.VMEM((2, rows, columns), F32),
            in_specs=[hbm] * 7,
            out_specs=vmem,
            scratch_shapes=[
                pltpu.SMEM(psf_columns.shape, F32),
                pltpu.SMEM(psf_rows.shape, F32),
                pltpu.SMEM(epoch_times.shape, jnp.int32),
                pltpu.SMEM(trial_rates.shape[::-1], jnp.int32),
                pltpu.VMEM(image, F32),
                pltpu.VMEM(image, F32),
                pltpu.VMEM(image, jnp.int32),
                pltpu.VMEM((epochs, 2, BAND, BAND), BF16),
                pltpu.VMEM((epochs, 2, 2, rows, columns + BAND), BF16),
                pltpu.VMEM((2, 2 * depth, columns + LANES), BF16),
                pltpu.VMEM((2, 2 * depth, columns), BF16),
                *pieces(groups),
                *pieces(groups),
                *pieces(groups),
                edge(far, 2, NEAR),
                edge(far, 2, NEAR),
                edge(far, 2, rows),
                edge(groups, 2, 2, PAD),
                edge(groups, 2, 2, PAD),
                edge(2, 2, NEAR),
                edge(2, 2, NEAR),
                dma((4,)),
                dma((epochs, 3)),
                dma((groups, 2, 2)),
                dma((groups, 2, 2)),
                dma((far, 2, 3)),
                dma((far, 2, 3)),
                dma((groups, 2, 2)),
                dma((groups, 2, 2)),
                dma((2, 2)),
                dma((2, 2)),
            ],
            compiler_params=pltpu.CompilerParams(collective_id=0, has_side_effects=True),
        )(flux_image, inv_var, pixel_mask, psf_columns, psf_rows, epoch_times, trial_rates.T)
        return stacks[:1], stacks[1:]

    in_specs = (
        P("epoch", "row", None),
        P("epoch", "row", None),
        P("epoch", "row", None),
        P("epoch", None),
        P("epoch", None),
        P("epoch"),
        P(),
    )
    out_specs = (P("epoch", "row", None), P("epoch", "row", None))
    return jax.shard_map(
        on_device, mesh=mesh, in_specs=in_specs, out_specs=out_specs, check_vma=False
    )
```

```python
import functools

import jax
import jax.numpy as jnp
from jax import lax
from jax.experimental import pallas as pl
from jax.experimental.pallas import tpu as pltpu
from jax.sharding import PartitionSpec as P

HALO = 8
PAD = 6
TSPAN = 64
TAPS = 2 * PAD + 1
LANES = 128
NEAR = 8
OVER = 3 * NEAR
EDGES = 2 * NEAR
BAND = 2 * LANES
FIELDS = (1, 0)
MESH = pl.DeviceIdType.MESH
F32 = jnp.float32
BF16 = jnp.bfloat16


def split(x):
    high = x.astype(BF16)
    return high, (x - high.astype(F32)).astype(BF16)


def iota(shape, axis):
    return lax.broadcasted_iota(jnp.int32, shape, axis)


def kernel(
    sizes,
    flux_hbm, inv_hbm, mask_hbm, psf_columns_hbm, psf_rows_hbm, times_hbm, rates_hbm,
    out,
    psf_columns, psf_rows, times, rates,
    flux, inv, mask, toeplitz, padded, convolved, shifted,
    pair_out, pair_in, own, far_in, near_out, near_in, row_out, row_in,
    small_sem, load_sem, pair_send, pair_recv, far_send, far_recv,
    near_send, near_recv, row_send, row_recv,
):
    groups, row_devices = sizes
    epochs, rows, columns = flux.shape
    tiles = columns // LANES
    depth = epochs * rows
    center = rows - EDGES
    me = lax.axis_index("epoch")
    core, group = lax.rem(me, 2), me // 2
    partner = me + 1 - 2 * core
    row = lax.axis_index("row")

    smalls = []
    for n, (src, dst) in enumerate((
        (psf_columns_hbm, psf_columns), (psf_rows_hbm, psf_rows), (times_hbm, times), (rates_hbm, rates),
    )):
        copy = pltpu.make_async_copy(src, dst, small_sem.at[n])
        copy.start()
        smalls.append(copy)
    loads = []
    for n, (src, dst) in enumerate(((inv_hbm, inv), (mask_hbm, mask), (flux_hbm, flux))):
        copy = pltpu.make_async_copy(src, dst, load_sem.at[n])
        copy.start()
        loads.append(copy)

    barrier = pltpu.get_barrier_semaphore()
    pl.semaphore_signal(barrier, inc=1, device_id={"epoch": partner}, device_id_type=MESH)
    for d in range(1, groups):
        there = 2 * lax.rem(group + d, groups) + core
        pl.semaphore_signal(barrier, inc=1, device_id={"epoch": there}, device_id_type=MESH)

    @pl.when(row > 0)
    def _():
        pl.semaphore_signal(barrier, inc=1, device_id={"row": row - 1}, device_id_type=MESH)

    @pl.when(row < row_devices - 1)
    def _():
        pl.semaphore_signal(barrier, inc=1, device_id={"row": row + 1}, device_id_type=MESH)

    for copy in smalls:
        copy.wait()
    offset = BAND // 4 - PAD - HALO
    tall = 2 * NEAR
    place = iota((tall, LANES), 0) - iota((tall, LANES), 1)
    wrapped = lax.rem(place - offset + 4 * LANES, LANES)
    for e in range(epochs):
        plain = jnp.zeros((tall, LANES), F32)
        for tap in range(TAPS):
            plain = jnp.where(wrapped == tap, psf_columns[e, tap], plain)
        for m in range(BAND // tall):
            turned = pltpu.roll(plain, (tall * m) % LANES, 1) if (tall * m) % LANES else plain
            where = place + (tall * m - offset)
            turned = jnp.where((where >= 0) & (where < TAPS), turned, 0.0)
            for f, value in enumerate((turned, turned * turned)):
                for n, piece in enumerate(split(value)):
                    toeplitz[e, f, m * tall : (m + 1) * tall, n * LANES : (n + 1) * LANES] = piece

    def shift(v, axis, e):
        return (rates[axis, v] * times[e]) >> (TSPAN.bit_length() - 1)

    def row_matrices(v):
        shape = (OVER + rows + NEAR, depth)
        o, k = iota(shape, 0), iota(shape, 1)
        far = jnp.where(rates[0, v] >= 0, -PAD - NEAR, rows + PAD)
        r = jnp.where(o < NEAR, o - PAD, o - NEAR + rows)
        r = jnp.where(o >= 2 * NEAR, o - 2 * NEAR + far, r)
        r = jnp.where(o >= OVER, o - OVER + NEAR, r)
        r = jnp.where(o >= OVER + center, o - OVER - center, r)
        r = jnp.where(o >= OVER + rows - NEAR, o - OVER, r)
        spare = (o >= OVER + rows) | ((o >= PAD) & (o < NEAR))
        spare = spare | ((o >= NEAR + PAD) & (o < 2 * NEAR))
        epoch_of = k // rows
        step = jnp.zeros(shape, jnp.int32)
        for e in range(epochs):
            step = jnp.where(epoch_of == e, shift(v, 0, e), step)
        at = r + step
        good = (at + row * rows >= 0) & (at + row * rows < rows * row_devices) & ~spare
        tap_at = jnp.where(good, lax.rem(k, rows) - at + PAD, -1)
        one_row = epoch_of[:1]
        plain = jnp.zeros(shape, F32)
        for tap in range(TAPS):
            value = jnp.zeros((1, depth), F32)
            for e in range(epochs):
                value = jnp.where(one_row == e, psf_rows[e, tap], value)
            plain = jnp.where(tap_at == tap, value, plain)
        stacks = []
        for value in (plain, plain * plain):
            high, low = split(value)
            both = jnp.concatenate([high, low], axis=0)
            stacks.append(jnp.concatenate([both, both], axis=1))
        return stacks

    half_lane = iota((rows, LANES), 1) < LANES // 2
    lane = iota((rows, LANES), 1)

    def prepare(e, f):
        field = inv[e] * mask[e].astype(F32)
        if f == 0:
            field = flux[e] * field
        turned = pltpu.roll(field, LANES // 2, 1)
        first = turned[:, :LANES]
        for n, piece in enumerate(split(turned)):
            padded[e, f, n, :, LANES:columns] = piece[:, LANES:]
        for n, piece in enumerate(split(jnp.where(half_lane, 0.0, first))):
            padded[e, f, n, :, :LANES] = piece
        for n, piece in enumerate(split(jnp.where(half_lane, first, 0.0))):
            padded[e, f, n, :, columns : columns + LANES] = piece
            padded[e, f, n, :, columns + LANES :] = jnp.zeros((rows, LANES), BF16)

    def convolve(e, f):
        windows = [
            padded[e, f, n, :, t * LANES : t * LANES + BAND] for n in range(2) for t in range(tiles + 1)
        ]
        result = jnp.dot(
            jnp.concatenate(windows, axis=0), toeplitz[e, f], preferred_element_type=F32
        )
        middle = (tiles + 1) * rows
        result = result[:middle, :LANES] + (result[:middle, LANES:] + result[middle:, :LANES])
        for t in range(tiles + 1):
            block = result[t * rows : (t + 1) * rows]
            if t == 0:
                block = jnp.where(lane >= HALO, block, 0.0)
            if t == tiles:
                block = jnp.where(lane < HALO, block, 0.0)
            for n, piece in enumerate(split(block)):
                at = slice(n * depth + e * rows, n * depth + (e + 1) * rows)
                convolved[f, at, t * LANES : (t + 1) * LANES] = piece

    def columns_stage(h, v, f):
        for e in range(epochs):
            step = shift(v, 1, e) + HALO
            stay = lane < LANES - step
            turn = lax.rem(LANES - step, LANES)
            for n in range(2):
                at = slice(n * depth + e * rows, n * depth + (e + 1) * rows)
                turned = [
                    pltpu.roll(convolved[f, at, t * LANES : (t + 1) * LANES], turn, 1)
                    for t in range(tiles + 1)
                ]
                for t in range(tiles):
                    shifted[h, at, t * LANES : (t + 1) * LANES] = jnp.where(stay, turned[t], turned[t + 1])

    def rows_stage(h, matrix):
        result = jnp.dot(matrix, shifted[h], preferred_element_type=F32)
        half = matrix.shape[0] // 2
        return result[:half] + result[half:]

    def pair_copy(*which):
        return pltpu.make_async_remote_copy(
            src_ref=pair_out.at[which], dst_ref=pair_in.at[which],
            send_sem=pair_send.at[0], recv_sem=pair_recv.at[which],
            device_id={"epoch": partner}, device_id_type=MESH,
        )

    parts = (slice(2 * NEAR, OVER), slice(OVER, OVER + center), slice(OVER + center, OVER + rows))

    def far_copy(d, f, part):
        return pltpu.make_async_remote_copy(
            src_ref=own.at[d, f, parts[part]],
            dst_ref=far_in.at[d - 1, f, parts[part]],
            send_sem=far_send.at[d - 1], recv_sem=far_recv.at[d - 1, f, part],
            device_id={"epoch": 2 * lax.rem(group + d, groups) + core}, device_id_type=MESH,
        )

    neighbours = ((row > 0, row - 1), (row < row_devices - 1, row + 1))

    def near_copy(d, f, way):
        return pltpu.make_async_remote_copy(
            src_ref=near_out.at[way, d, f], dst_ref=near_in.at[way, d, f],
            send_sem=near_send.at[way], recv_sem=near_recv.at[way, d, f],
            device_id={"row": neighbours[way][1]}, device_id_type=MESH,
        )

    def row_copy(f, way):
        return pltpu.make_async_remote_copy(
            src_ref=row_out.at[way, f], dst_ref=row_in.at[way, f],
            send_sem=row_send.at[way], recv_sem=row_recv.at[way, f],
            device_id={"row": neighbours[way][1]}, device_id_type=MESH,
        )

    def to_neighbours(copy_of, *which):
        odd = lax.rem(row, 2)
        for way, turn in ((1, odd == 1), (0, True), (1, odd == 0)):
            @pl.when(neighbours[way][0] & turn)
            def _():
                copy_of(*which, way).start()

    def from_neighbours(copy_of, which, add):
        for way in range(2):
            @pl.when(neighbours[1 - way][0])
            def _():
                copy_of(*which, way).wait_recv()
                add(way)

    def finish(d, f):
        pair_copy(d, f).wait_recv()
        total = own[d, f] + pair_in[d, f]
        own[d, f, 2 * NEAR :] = total[2 * NEAR :]
        if d:
            far_copy(d, f, 0).start()
        for way in range(2):
            near_out[way, d, f] = total[way * NEAR : way * NEAR + PAD]
        to_neighbours(near_copy, d, f)
        if d:
            far_copy(d, f, 1).start()

    def finish_edges(d, f):
        def add(way):
            at = slice(OVER + rows - PAD, OVER + rows) if way == 0 else slice(OVER + center, OVER + center + PAD)
            own[d, f, at] = own[d, f, at] + near_in[way, d, f]

        from_neighbours(near_copy, (d, f), add)
        far_copy(d, f, 2).start()

    def pair_of(d):
        goal = 2 * lax.rem(group + d, groups)
        return goal + 1 - core, goal + core

    order = (*range(1, groups), 0)
    items = [(d, f) for d in order for f in FIELDS]
    matrices = [row_matrices(v) for v in pair_of(order[0])]
    for n, (d, f) in enumerate(items):
        pair = pair_of(d)
        if n < 2:
            for copy in loads[:2] if n == 0 else loads[2:]:
                copy.wait()
            for e in range(epochs):
                prepare(e, f)
            for e in range(epochs):
                convolve(e, f)
        elif f == FIELDS[0]:
            matrices = [row_matrices(v) for v in pair]
        for h in range(2):
            columns_stage(h, pair[h], f)
        part, own_part = (rows_stage(h, matrices[h][f]) for h in range(2))
        own[d, f] = own_part[: OVER + rows]
        if n == 0:
            above = lax.div(row + row_devices - 1, row_devices)
            below = lax.div(2 * row_devices - 2 - row, row_devices)
            pl.semaphore_wait(barrier, groups + above + below)
        pair_out[d, f] = part[: OVER + rows]
        pair_copy(d, f).start()
        if n:
            finish(*items[n - 1])
    finish(*items[-1])
    for item in items:
        if item[0]:
            finish_edges(*item)

    upward = rates[0, me] >= 0
    for f in FIELDS:
        far = own[0, f, parts[0]]
        for d in range(1, groups):
            far_copy(d, f, 0).wait_recv()
            far = far + far_in[d - 1, f, parts[0]]
        row_out[0, f] = jnp.where(upward, far, 0.0)
        row_out[1, f] = jnp.where(upward, 0.0, far)
        to_neighbours(row_copy, f)

    def add_to(f, at, value):
        out[f, at] = out[f, at] + value

    for f in FIELDS:
        total = own[0, f, OVER:]
        out[f, NEAR : rows - NEAR] = total[:center]
        out[f, :NEAR] = total[center : center + NEAR]
        out[f, rows - NEAR :] = total[center + NEAR :]
        from_neighbours(near_copy, (0, f), lambda way: add_to(
            f, slice(rows - PAD, rows) if way == 0 else slice(0, PAD), near_in[way, 0, f]
        ))
    for f in FIELDS:
        for d in range(1, groups):
            far_copy(d, f, 1).wait_recv()
            add_to(f, slice(NEAR, rows - NEAR), far_in[d - 1, f, parts[1]])
    for f in FIELDS:
        from_neighbours(row_copy, (f,), lambda way: add_to(
            f, slice(rows - PAD - NEAR, rows - PAD) if way == 0 else slice(PAD, PAD + NEAR), row_in[way, f]
        ))
        for d in range(1, groups):
            far_copy(d, f, 2).wait_recv()
            edges = far_in[d - 1, f, parts[2]]
            add_to(f, slice(0, NEAR), edges[:NEAR])
            add_to(f, slice(rows - NEAR, rows), edges[NEAR:])

    def wait_sent(src, sem):
        pltpu.make_async_copy(src, src, sem).wait()

    wait_sent(pair_out, pair_send.at[0])
    for d in range(1, groups):
        wait_sent(own.at[d, :, 2 * NEAR :], far_send.at[d - 1])
    for way in range(2):
        @pl.when(neighbours[way][0])
        def _():
            wait_sent(near_out.at[way], near_send.at[way])
            wait_sent(row_out.at[way], row_send.at[way])


def solution(mesh):
    epoch_devices, row_devices = mesh.shape["epoch"], mesh.shape["row"]
    groups = epoch_devices // 2

    def on_device(flux_image, inv_var, pixel_mask, psf_columns, psf_rows, epoch_times, trial_rates):
        epochs, rows, columns = flux_image.shape
        depth = epochs * rows
        assert epoch_devices % 2 == 0 and trial_rates.shape[0] == epoch_devices
        assert rows % (2 * NEAR) == 0 and rows > 2 * NEAR and columns % LANES == 0 and depth % LANES == 0
        far = max(groups - 1, 1)
        hbm = pl.BlockSpec(memory_space=pl.ANY)
        vmem = pl.BlockSpec(memory_space=pltpu.VMEM)
        image = (epochs, rows, columns)

        def buffer(*size):
            return pltpu.VMEM((*size, columns), F32)

        block = OVER + rows
        dma = pltpu.SemaphoreType.DMA
        stacks = pl.pallas_call(
            functools.partial(kernel, (groups, row_devices)),
            out_shape=pltpu.VMEM((2, rows, columns), F32),
            in_specs=[hbm] * 7,
            out_specs=vmem,
            scratch_shapes=[
                pltpu.SMEM(psf_columns.shape, F32),
                pltpu.SMEM(psf_rows.shape, F32),
                pltpu.SMEM(epoch_times.shape, jnp.int32),
                pltpu.SMEM(trial_rates.shape[::-1], jnp.int32),
                pltpu.VMEM(image, F32),
                pltpu.VMEM(image, F32),
                pltpu.VMEM(image, jnp.int32),
                pltpu.VMEM((epochs, 2, BAND, BAND), BF16),
                pltpu.VMEM((epochs, 2, 2, rows, columns + BAND), BF16),
                pltpu.VMEM((2, 2 * depth, columns + LANES), BF16),
                pltpu.VMEM((2, 2 * depth, columns), BF16),
                buffer(groups, 2, block),
                buffer(groups, 2, block),
                buffer(groups, 2, block),
                buffer(far, 2, block),
                buffer(2, groups, 2, PAD),
                buffer(2, groups, 2, PAD),
                buffer(2, 2, NEAR),
                buffer(2, 2, NEAR),
                dma((4,)),
                dma((3,)),
                dma((1,)),
                dma((groups, 2)),
                dma((far,)),
                dma((far, 2, 3)),
                dma((2,)),
                dma((2, groups, 2)),
                dma((2,)),
                dma((2, 2)),
            ],
            compiler_params=pltpu.CompilerParams(collective_id=0, has_side_effects=True),
        )(flux_image, inv_var, pixel_mask, psf_columns, psf_rows, epoch_times, trial_rates.T)
        return stacks[:1], stacks[1:]

    in_specs = (
        P("epoch", "row", None),
        P("epoch", "row", None),
        P("epoch", "row", None),
        P("epoch", None),
        P("epoch", None),
        P("epoch"),
        P(),
    )
    out_specs = (P("epoch", "row", None), P("epoch", "row", None))
    return jax.shard_map(
        on_device, mesh=mesh, in_specs=in_specs, out_specs=out_specs, check_vma=False
    )
```

```python
import functools

import jax
import jax.numpy as jnp
from jax import lax
from jax.experimental import pallas as pl
from jax.experimental.pallas import tpu as pltpu
from jax.sharding import PartitionSpec as P

HALO = 8
PAD = 6
TSPAN = 64
TAPS = 2 * PAD + 1
LANES = 128
NEAR = 8
OVER = 3 * NEAR
EDGES = 2 * NEAR
BAND = 2 * LANES
FIELDS = (1, 0)
FIRST, LATER = FIELDS
MESH = pl.DeviceIdType.MESH
F32 = jnp.float32
BF16 = jnp.bfloat16


def split(x):
    high = x.astype(BF16)
    return high, (x - high.astype(F32)).astype(BF16)


def iota(shape, axis):
    return lax.broadcasted_iota(jnp.int32, shape, axis)


def kernel(
    sizes,
    flux_hbm, inv_hbm, mask_hbm, psf_columns_hbm, psf_rows_hbm, times_hbm, rates_hbm,
    out,
    psf_columns, psf_rows, times, rates,
    flux, inv, mask, toeplitz, padded, convolved, shifted,
    pair_out, pair_in, own, far_in, cross_in, near_out, near_in, row_out, row_in, up_out, up_in,
    small_sem, load_sem, pair_send, pair_recv, far_send, far_recv,
    near_send, near_recv, row_send, row_recv, up_send, cross_send, cross_recv,
):
    groups, row_devices = sizes
    epochs, rows, columns = flux.shape
    tiles = columns // LANES
    depth = epochs * rows
    center = rows - EDGES
    me = lax.axis_index("epoch")
    core, group = lax.rem(me, 2), me // 2
    partner = me + 1 - 2 * core
    row = lax.axis_index("row")

    smalls = []
    for n, (src, dst) in enumerate((
        (psf_columns_hbm, psf_columns), (psf_rows_hbm, psf_rows), (times_hbm, times), (rates_hbm, rates),
    )):
        copy = pltpu.make_async_copy(src, dst, small_sem.at[n])
        copy.start()
        smalls.append(copy)
    loads = []
    for n, (src, dst) in enumerate(((inv_hbm, inv), (mask_hbm, mask), (flux_hbm, flux))):
        copy = pltpu.make_async_copy(src, dst, load_sem.at[n])
        copy.start()
        loads.append(copy)

    barrier = pltpu.get_barrier_semaphore()
    pl.semaphore_signal(barrier, inc=1, device_id={"epoch": partner}, device_id_type=MESH)
    for d in range(1, groups):
        there = 2 * lax.rem(group + d, groups)
        for c in range(2):
            pl.semaphore_signal(barrier, inc=1, device_id={"epoch": there + c}, device_id_type=MESH)

    @pl.when(row > 0)
    def _():
        pl.semaphore_signal(barrier, inc=1, device_id={"row": row - 1}, device_id_type=MESH)

    @pl.when(row < row_devices - 1)
    def _():
        pl.semaphore_signal(barrier, inc=1, device_id={"row": row + 1}, device_id_type=MESH)

    for copy in smalls:
        copy.wait()
    offset = BAND // 4 - PAD - HALO
    tall = 2 * NEAR
    place = iota((tall, LANES), 0) - iota((tall, LANES), 1)
    wrapped = lax.rem(place - offset + 4 * LANES, LANES)
    for e in range(epochs):
        plain = jnp.zeros((tall, LANES), F32)
        for tap in range(TAPS):
            plain = jnp.where(wrapped == tap, psf_columns[e, tap], plain)
        for m in range(BAND // tall):
            turned = pltpu.roll(plain, (tall * m) % LANES, 1) if (tall * m) % LANES else plain
            where = place + (tall * m - offset)
            turned = jnp.where((where >= 0) & (where < TAPS), turned, 0.0)
            for f, value in enumerate((turned, turned * turned)):
                for n, piece in enumerate(split(value)):
                    toeplitz[e, f, m * tall : (m + 1) * tall, n * LANES : (n + 1) * LANES] = piece

    def shift(v, axis, e):
        return (rates[axis, v] * times[e]) >> (TSPAN.bit_length() - 1)

    def row_matrices(v):
        shape = (OVER + rows + NEAR, depth)
        o, k = iota(shape, 0), iota(shape, 1)
        far = jnp.where(rates[0, v] >= 0, -PAD - NEAR, rows + PAD)
        r = jnp.where(o < NEAR, o + rows, o - NEAR - PAD)
        r = jnp.where(o >= 2 * NEAR, o - 2 * NEAR + far, r)
        r = jnp.where(o >= OVER, o - OVER + NEAR, r)
        r = jnp.where(o >= OVER + center, o - OVER - center, r)
        r = jnp.where(o >= OVER + rows - NEAR, o - OVER, r)
        spare = (o >= OVER + rows) | ((o >= PAD) & (o < NEAR))
        spare = spare | ((o >= NEAR + PAD) & (o < 2 * NEAR))
        epoch_of = k // rows
        step = jnp.zeros(shape, jnp.int32)
        for e in range(epochs):
            step = jnp.where(epoch_of == e, shift(v, 0, e), step)
        at = r + step
        good = (at + row * rows >= 0) & (at + row * rows < rows * row_devices) & ~spare
        tap_at = jnp.where(good, lax.rem(k, rows) - at + PAD, -1)
        one_row = epoch_of[:1]
        plain = jnp.zeros(shape, F32)
        for tap in range(TAPS):
            value = jnp.zeros((1, depth), F32)
            for e in range(epochs):
                value = jnp.where(one_row == e, psf_rows[e, tap], value)
            plain = jnp.where(tap_at == tap, value, plain)
        stacks = []
        for value in (plain, plain * plain):
            high, low = split(value)
            both = jnp.concatenate([high, low], axis=0)
            stacks.append(jnp.concatenate([both, both], axis=1))
        return stacks

    half_lane = iota((rows, LANES), 1) < LANES // 2
    lane = iota((rows, LANES), 1)

    def prepare(e, f):
        field = inv[e] * mask[e].astype(F32)
        if f == 0:
            field = flux[e] * field
        turned = pltpu.roll(field, LANES // 2, 1)
        first = turned[:, :LANES]
        for n, piece in enumerate(split(turned)):
            padded[e, f, n, :, LANES:columns] = piece[:, LANES:]
        for n, piece in enumerate(split(jnp.where(half_lane, 0.0, first))):
            padded[e, f, n, :, :LANES] = piece
        for n, piece in enumerate(split(jnp.where(half_lane, first, 0.0))):
            padded[e, f, n, :, columns : columns + LANES] = piece
            padded[e, f, n, :, columns + LANES :] = jnp.zeros((rows, LANES), BF16)

    def convolve(e, f):
        windows = [
            padded[e, f, n, :, t * LANES : t * LANES + BAND] for n in range(2) for t in range(tiles + 1)
        ]
        result = jnp.dot(
            jnp.concatenate(windows, axis=0), toeplitz[e, f], preferred_element_type=F32
        )
        middle = (tiles + 1) * rows
        result = result[:middle, :LANES] + (result[:middle, LANES:] + result[middle:, :LANES])
        for t in range(tiles + 1):
            block = result[t * rows : (t + 1) * rows]
            if t == 0:
                block = jnp.where(lane >= HALO, block, 0.0)
            if t == tiles:
                block = jnp.where(lane < HALO, block, 0.0)
            for n, piece in enumerate(split(block)):
                at = slice(n * depth + e * rows, n * depth + (e + 1) * rows)
                convolved[f, at, t * LANES : (t + 1) * LANES] = piece

    def columns_stage(h, v, f):
        for e in range(epochs):
            step = shift(v, 1, e) + HALO
            stay = lane < LANES - step
            turn = lax.rem(LANES - step, LANES)
            for n in range(2):
                at = slice(n * depth + e * rows, n * depth + (e + 1) * rows)
                turned = [
                    pltpu.roll(convolved[f, at, t * LANES : (t + 1) * LANES], turn, 1)
                    for t in range(tiles + 1)
                ]
                for t in range(tiles):
                    shifted[h, at, t * LANES : (t + 1) * LANES] = jnp.where(stay, turned[t], turned[t + 1])

    def rows_stage(h, matrix):
        result = jnp.dot(matrix, shifted[h], preferred_element_type=F32)
        half = matrix.shape[0] // 2
        return result[:half] + result[half:]

    def pair_copy(d, f, part):
        at = slice(part * OVER, OVER + part * rows)
        return pltpu.make_async_remote_copy(
            src_ref=pair_out.at[d, f, at], dst_ref=pair_in.at[d, f, at],
            send_sem=pair_send.at[0], recv_sem=pair_recv.at[d, f, part],
            device_id={"epoch": partner}, device_id_type=MESH,
        )

    def far_rows(f):
        return slice(NEAR if f == LATER else 2 * NEAR, OVER)

    center_rows, edge_rows = slice(OVER, OVER + center), slice(OVER + center, OVER + rows)

    def far_copy(d, f, part, short=False):
        at = (slice(2 * NEAR, OVER) if short else far_rows(f), center_rows, edge_rows)[part]
        return pltpu.make_async_remote_copy(
            src_ref=own.at[d, f, at], dst_ref=far_in.at[d - 1, f, at],
            send_sem=far_send.at[d - 1, f], recv_sem=far_recv.at[d - 1, f, part],
            device_id={"epoch": 2 * lax.rem(group + d, groups) + core}, device_id_type=MESH,
        )

    def over_copy(d, act):
        @pl.when(row > 0)
        def _():
            act(far_copy(d, LATER, 0))

        @pl.when(row == 0)
        def _():
            act(far_copy(d, LATER, 0, True))

    def cross_copy(d):
        return pltpu.make_async_remote_copy(
            src_ref=pair_out.at[d, FIRST, far_rows(FIRST)], dst_ref=cross_in.at[d - 1],
            send_sem=cross_send.at[d - 1], recv_sem=cross_recv.at[d - 1],
            device_id={"epoch": 2 * lax.rem(group + d, groups) + 1 - core}, device_id_type=MESH,
        )

    neighbours = ((row > 0, row - 1), (row < row_devices - 1, row + 1))

    def near_copy(d, f, way):
        return pltpu.make_async_remote_copy(
            src_ref=near_out.at[way, d, f], dst_ref=near_in.at[way, d, f],
            send_sem=near_send.at[way], recv_sem=near_recv.at[way, d, f],
            device_id={"row": neighbours[way][1]}, device_id_type=MESH,
        )

    def row_copy(f, way):
        if f == LATER and way == 0:
            return pltpu.make_async_remote_copy(
                src_ref=up_out, dst_ref=up_in, send_sem=up_send.at[0], recv_sem=row_recv.at[0, f],
                device_id={"row": neighbours[0][1]}, device_id_type=MESH,
            )
        return pltpu.make_async_remote_copy(
            src_ref=row_out.at[way, f], dst_ref=row_in.at[way, f],
            send_sem=row_send.at[way], recv_sem=row_recv.at[way, f],
            device_id={"row": neighbours[way][1]}, device_id_type=MESH,
        )

    def near_ways(f):
        return (1,) if f == LATER else (0, 1)

    def to_neighbours(copy_of, *which, ways=(0, 1)):
        for way in ways:
            @pl.when(neighbours[way][0])
            def _():
                copy_of(*which, way).start()

    def from_neighbours(copy_of, which, add, ways=(0, 1)):
        for way in ways:
            @pl.when(neighbours[1 - way][0])
            def _():
                copy_of(*which, way).wait_recv()
                add(way)

    def finish(d, f):
        pair_copy(d, f, 0).wait_recv()
        total = own[d, f, :OVER] + pair_in[d, f, :OVER]
        if not d or f == LATER:
            own[d, f, NEAR:OVER] = total[NEAR:]
        if d and f == LATER:
            over_copy(d, lambda copy: copy.start())
        for way in near_ways(f):
            at = (1 - way) * NEAR
            near_out[way, d, f] = total[at : at + PAD]
        to_neighbours(near_copy, d, f, ways=near_ways(f))
        pair_copy(d, f, 1).wait_recv()
        own[d, f, OVER:] = own[d, f, OVER:] + pair_in[d, f, OVER:]
        if d:
            far_copy(d, f, 1).start()

    def finish_edges(d, f):
        def add(way):
            at = slice(OVER + rows - PAD, OVER + rows) if way == 0 else slice(OVER + center, OVER + center + PAD)
            own[d, f, at] = own[d, f, at] + near_in[way, d, f]

        from_neighbours(near_copy, (d, f), add, near_ways(f))
        far_copy(d, f, 2).start()

    def pair_of(d):
        goal = 2 * lax.rem(group + d, groups)
        return goal + 1 - core, goal + core

    order = (*range(1, groups), 0)
    items = [(d, f) for d in order for f in FIELDS]
    matrices = [row_matrices(v) for v in pair_of(order[0])]
    for n, (d, f) in enumerate(items):
        pair = pair_of(d)
        if n < 2:
            for copy in loads[:2] if n == 0 else loads[2:]:
                copy.wait()
            for e in range(epochs):
                prepare(e, f)
            for e in range(epochs):
                convolve(e, f)
        elif f == FIRST:
            matrices = [row_matrices(v) for v in pair]
        for h in range(2):
            columns_stage(h, pair[h], f)
        part, own_part = (rows_stage(h, matrices[h][f]) for h in range(2))
        own[d, f] = own_part[: OVER + rows]
        if n == 0:
            above = lax.div(row + row_devices - 1, row_devices)
            below = lax.div(2 * row_devices - 2 - row, row_devices)
            pl.semaphore_wait(barrier, 2 * groups - 1 + above + below)
        pair_out[d, f] = part[: OVER + rows]
        for part in range(2):
            pair_copy(d, f, part).start()
        if d and f == FIRST:
            far_copy(d, f, 0).start()
            cross_copy(d).start()
        if n:
            finish(*items[n - 1])
    finish(*items[-1])
    upward = rates[0, me] >= 0
    for d in range(1, groups):
        finish_edges(d, FIRST)
    for f in FIELDS:
        far = own[0, f, far_rows(f)]
        for d in range(1, groups):
            if f == LATER:
                over_copy(d, lambda copy: copy.wait_recv())
            else:
                far_copy(d, f, 0).wait_recv()
            far = far + far_in[d - 1, f, far_rows(f)]
            if f == FIRST:
                cross_copy(d).wait_recv()
                far = far + cross_in[d - 1]
        if f == LATER:
            up_out[NEAR:] = far[:PAD]
            far = far[NEAR:]
            up_out[:NEAR] = jnp.where(upward, far, 0.0)
        else:
            row_out[0, f] = jnp.where(upward, far, 0.0)
        row_out[1, f] = jnp.where(upward, 0.0, far)
        to_neighbours(row_copy, f)

    for d in range(1, groups):
        finish_edges(d, LATER)

    def add_to(f, at, value):
        out[f, at] = out[f, at] + value

    for f in FIELDS:
        total = own[0, f, OVER:]
        out[f, NEAR : rows - NEAR] = total[:center]
        out[f, :NEAR] = total[center : center + NEAR]
        out[f, rows - NEAR :] = total[center + NEAR :]
        from_neighbours(near_copy, (0, f), lambda way: add_to(
            f, slice(rows - PAD, rows) if way == 0 else slice(0, PAD), near_in[way, 0, f]
        ), near_ways(f))
    for f in FIELDS:
        for d in range(1, groups):
            far_copy(d, f, 1).wait_recv()
            add_to(f, slice(NEAR, rows - NEAR), far_in[d - 1, f, center_rows])
    for f in FIELDS:
        def add_far(way):
            if way == 1:
                add_to(f, slice(PAD, PAD + NEAR), row_in[1, f])
            elif f == LATER:
                add_to(f, slice(rows - PAD - NEAR, rows), up_in[...])
            else:
                add_to(f, slice(rows - PAD - NEAR, rows - PAD), row_in[0, f])

        from_neighbours(row_copy, (f,), add_far)
        for d in range(1, groups):
            far_copy(d, f, 2).wait_recv()
            edges = far_in[d - 1, f, edge_rows]
            add_to(f, slice(0, NEAR), edges[:NEAR])
            add_to(f, slice(rows - NEAR, rows), edges[NEAR:])

    def wait_sent(src, sem):
        pltpu.make_async_copy(src, src, sem).wait()

    wait_sent(pair_out, pair_send.at[0])
    for d in range(1, groups):
        wait_sent(own.at[d, FIRST, 2 * NEAR :], far_send.at[d - 1, FIRST])

        @pl.when(row > 0)
        def _():
            wait_sent(own.at[d, LATER, NEAR:], far_send.at[d - 1, LATER])

        @pl.when(row == 0)
        def _():
            wait_sent(own.at[d, LATER, 2 * NEAR :], far_send.at[d - 1, LATER])


        cross_copy(d).wait_send()

    @pl.when(neighbours[0][0])
    def _():
        wait_sent(near_out.at[0, :, FIRST], near_send.at[0])
        row_copy(FIRST, 0).wait_send()
        row_copy(LATER, 0).wait_send()

    @pl.when(neighbours[1][0])
    def _():
        wait_sent(near_out.at[1], near_send.at[1])
        wait_sent(row_out.at[1], row_send.at[1])


def solution(mesh):
    epoch_devices, row_devices = mesh.shape["epoch"], mesh.shape["row"]
    groups = epoch_devices // 2

    def on_device(flux_image, inv_var, pixel_mask, psf_columns, psf_rows, epoch_times, trial_rates):
        epochs, rows, columns = flux_image.shape
        depth = epochs * rows
        assert epoch_devices % 2 == 0 and trial_rates.shape[0] == epoch_devices
        assert rows % (2 * NEAR) == 0 and rows > 2 * NEAR and columns % LANES == 0 and depth % LANES == 0
        far = max(groups - 1, 1)
        hbm = pl.BlockSpec(memory_space=pl.ANY)
        vmem = pl.BlockSpec(memory_space=pltpu.VMEM)
        image = (epochs, rows, columns)

        def buffer(*size):
            return pltpu.VMEM((*size, columns), F32)

        block = OVER + rows
        dma = pltpu.SemaphoreType.DMA
        stacks = pl.pallas_call(
            functools.partial(kernel, (groups, row_devices)),
            out_shape=pltpu.VMEM((2, rows, columns), F32),
            in_specs=[hbm] * 7,
            out_specs=vmem,
            scratch_shapes=[
                pltpu.SMEM(psf_columns.shape, F32),
                pltpu.SMEM(psf_rows.shape, F32),
                pltpu.SMEM(epoch_times.shape, jnp.int32),
                pltpu.SMEM(trial_rates.shape[::-1], jnp.int32),
                pltpu.VMEM(image, F32),
                pltpu.VMEM(image, F32),
                pltpu.VMEM(image, jnp.int32),
                pltpu.VMEM((epochs, 2, BAND, BAND), BF16),
                pltpu.VMEM((epochs, 2, 2, rows, columns + BAND), BF16),
                pltpu.VMEM((2, 2 * depth, columns + LANES), BF16),
                pltpu.VMEM((2, 2 * depth, columns), BF16),
                buffer(groups, 2, block),
                buffer(groups, 2, block),
                buffer(groups, 2, block),
                buffer(far, 2, block),
                buffer(far, NEAR),
                buffer(2, groups, 2, PAD),
                buffer(2, groups, 2, PAD),
                buffer(2, 2, NEAR),
                buffer(2, 2, NEAR),
                buffer(NEAR + PAD),
                buffer(NEAR + PAD),
                dma((4,)),
                dma((3,)),
                dma((1,)),
                dma((groups, 2, 2)),
                dma((far, 2)),
                dma((far, 2, 3)),
                dma((2,)),
                dma((2, groups, 2)),
                dma((2,)),
                dma((2, 2)),
                dma((1,)),
                dma((far,)),
                dma((far,)),
            ],
            compiler_params=pltpu.CompilerParams(collective_id=0, has_side_effects=True),
        )(flux_image, inv_var, pixel_mask, psf_columns, psf_rows, epoch_times, trial_rates.T)
        return stacks[:1], stacks[1:]

    in_specs = (
        P("epoch", "row", None),
        P("epoch", "row", None),
        P("epoch", "row", None),
        P("epoch", None),
        P("epoch", None),
        P("epoch"),
        P(),
    )
    out_specs = (P("epoch", "row", None), P("epoch", "row", None))
    return jax.shard_map(
        on_device, mesh=mesh, in_specs=in_specs, out_specs=out_specs, check_vma=False
    )
```

```python
import functools

import jax
import jax.numpy as jnp
from jax import lax
from jax.experimental import pallas as pl
from jax.experimental.pallas import tpu as pltpu
from jax.sharding import PartitionSpec as P

HALO = 8
PAD = 6
TSPAN = 64
TAPS = 2 * PAD + 1
LANES = 128
NEAR = 8
OVER = 3 * NEAR
EDGES = 2 * NEAR
BAND = 2 * LANES
FIELDS = (1, 0)
FIRST, LATER = FIELDS
MESH = pl.DeviceIdType.MESH
F32 = jnp.float32
BF16 = jnp.bfloat16


def split(x):
    high = x.astype(BF16)
    return high, (x - high.astype(F32)).astype(BF16)


def iota(shape, axis):
    return lax.broadcasted_iota(jnp.int32, shape, axis)


def kernel(
    sizes,
    flux_hbm, inv_hbm, mask_hbm, psf_columns_hbm, psf_rows_hbm, times_hbm, rates_hbm,
    out,
    psf_columns, psf_rows, times, rates,
    flux, inv, mask, toeplitz, padded, convolved, shifted,
    pair_out, pair_in, own, far_in, cross_in, near_out, near_in, row_out, row_in, up_out, up_in,
    small_sem, load_sem, pair_send, pair_recv, far_send, far_recv,
    near_send, near_recv, row_send, row_recv, up_send, cross_send, cross_recv,
):
    groups, row_devices = sizes
    epochs, rows, columns = flux.shape
    tiles = columns // LANES
    depth = epochs * rows
    center = rows - EDGES
    me = lax.axis_index("epoch")
    core, group = lax.rem(me, 2), me // 2
    partner = me + 1 - 2 * core
    row = lax.axis_index("row")

    smalls = []
    for n, (src, dst) in enumerate((
        (psf_columns_hbm, psf_columns), (psf_rows_hbm, psf_rows), (times_hbm, times), (rates_hbm, rates),
    )):
        copy = pltpu.make_async_copy(src, dst, small_sem.at[n])
        copy.start()
        smalls.append(copy)
    loads = []
    for n, (src, dst) in enumerate(((inv_hbm, inv), (mask_hbm, mask), (flux_hbm, flux))):
        copy = pltpu.make_async_copy(src, dst, load_sem.at[n])
        copy.start()
        loads.append(copy)

    barrier = pltpu.get_barrier_semaphore()
    pl.semaphore_signal(barrier, inc=1, device_id={"epoch": partner}, device_id_type=MESH)
    for d in range(1, groups):
        there = 2 * lax.rem(group + d, groups)
        for c in range(2):
            pl.semaphore_signal(barrier, inc=1, device_id={"epoch": there + c}, device_id_type=MESH)

    @pl.when(row > 0)
    def _():
        pl.semaphore_signal(barrier, inc=1, device_id={"row": row - 1}, device_id_type=MESH)

    @pl.when(row < row_devices - 1)
    def _():
        pl.semaphore_signal(barrier, inc=1, device_id={"row": row + 1}, device_id_type=MESH)

    for copy in smalls:
        copy.wait()
    offset = BAND // 4 - PAD - HALO
    tall = 2 * NEAR
    place = iota((tall, LANES), 0) - iota((tall, LANES), 1)
    wrapped = lax.rem(place - offset + 4 * LANES, LANES)
    for e in range(epochs):
        plain = jnp.zeros((tall, LANES), F32)
        for tap in range(TAPS):
            plain = jnp.where(wrapped == tap, psf_columns[e, tap], plain)
        for m in range(BAND // tall):
            turned = pltpu.roll(plain, (tall * m) % LANES, 1) if (tall * m) % LANES else plain
            where = place + (tall * m - offset)
            turned = jnp.where((where >= 0) & (where < TAPS), turned, 0.0)
            for f, value in enumerate((turned, turned * turned)):
                for n, piece in enumerate(split(value)):
                    toeplitz[e, f, m * tall : (m + 1) * tall, n * LANES : (n + 1) * LANES] = piece

    def shift(v, axis, e):
        return (rates[axis, v] * times[e]) >> (TSPAN.bit_length() - 1)

    def row_matrices(v):
        shape = (OVER + rows + NEAR, depth)
        o, k = iota(shape, 0), iota(shape, 1)
        far = jnp.where(rates[0, v] >= 0, -PAD - NEAR, rows + PAD)
        r = jnp.where(o < NEAR, o + rows, o - NEAR - PAD)
        r = jnp.where(o >= 2 * NEAR, o - 2 * NEAR + far, r)
        r = jnp.where(o >= OVER, o - OVER + NEAR, r)
        r = jnp.where(o >= OVER + center, o - OVER - center, r)
        r = jnp.where(o >= OVER + rows - NEAR, o - OVER, r)
        spare = (o >= OVER + rows) | ((o >= PAD) & (o < NEAR))
        spare = spare | ((o >= NEAR + PAD) & (o < 2 * NEAR))
        epoch_of = k // rows
        step = jnp.zeros(shape, jnp.int32)
        for e in range(epochs):
            step = jnp.where(epoch_of == e, shift(v, 0, e), step)
        at = r + step
        good = (at + row * rows >= 0) & (at + row * rows < rows * row_devices) & ~spare
        tap_at = jnp.where(good, lax.rem(k, rows) - at + PAD, -1)
        one_row = epoch_of[:1]
        plain = jnp.zeros(shape, F32)
        for tap in range(TAPS):
            value = jnp.zeros((1, depth), F32)
            for e in range(epochs):
                value = jnp.where(one_row == e, psf_rows[e, tap], value)
            plain = jnp.where(tap_at == tap, value, plain)
        stacks = []
        for value in (plain, plain * plain):
            high, low = split(value)
            both = jnp.concatenate([high, low], axis=0)
            stacks.append(jnp.concatenate([both, both], axis=1))
        return stacks

    half_lane = iota((rows, LANES), 1) < LANES // 2
    lane = iota((rows, LANES), 1)

    def prepare(e, f):
        field = inv[e] * mask[e].astype(F32)
        if f == 0:
            field = flux[e] * field
        turned = pltpu.roll(field, LANES // 2, 1)
        first = turned[:, :LANES]
        for n, piece in enumerate(split(turned)):
            padded[e, f, n, :, LANES:columns] = piece[:, LANES:]
        for n, piece in enumerate(split(jnp.where(half_lane, 0.0, first))):
            padded[e, f, n, :, :LANES] = piece
        for n, piece in enumerate(split(jnp.where(half_lane, first, 0.0))):
            padded[e, f, n, :, columns : columns + LANES] = piece
            padded[e, f, n, :, columns + LANES :] = jnp.zeros((rows, LANES), BF16)

    def convolve(e, f):
        windows = [
            padded[e, f, n, :, t * LANES : t * LANES + BAND] for n in range(2) for t in range(tiles + 1)
        ]
        result = jnp.dot(
            jnp.concatenate(windows, axis=0), toeplitz[e, f], preferred_element_type=F32
        )
        middle = (tiles + 1) * rows
        result = result[:middle, :LANES] + (result[:middle, LANES:] + result[middle:, :LANES])
        for t in range(tiles + 1):
            block = result[t * rows : (t + 1) * rows]
            if t == 0:
                block = jnp.where(lane >= HALO, block, 0.0)
            if t == tiles:
                block = jnp.where(lane < HALO, block, 0.0)
            for n, piece in enumerate(split(block)):
                at = slice(n * depth + e * rows, n * depth + (e + 1) * rows)
                convolved[f, at, t * LANES : (t + 1) * LANES] = piece

    def columns_stage(h, v, f):
        for e in range(epochs):
            step = shift(v, 1, e) + HALO
            stay = lane < LANES - step
            turn = lax.rem(LANES - step, LANES)
            for n in range(2):
                at = slice(n * depth + e * rows, n * depth + (e + 1) * rows)
                turned = [
                    pltpu.roll(convolved[f, at, t * LANES : (t + 1) * LANES], turn, 1)
                    for t in range(tiles + 1)
                ]
                for t in range(tiles):
                    shifted[h, at, t * LANES : (t + 1) * LANES] = jnp.where(stay, turned[t], turned[t + 1])

    def rows_stage(h, matrix):
        result = jnp.dot(matrix, shifted[h], preferred_element_type=F32)
        half = matrix.shape[0] // 2
        return result[:half] + result[half:]

    def pair_copy(d, f, part):
        at = slice(part * OVER, OVER + part * rows)
        return pltpu.make_async_remote_copy(
            src_ref=pair_out.at[d, f, at], dst_ref=pair_in.at[d, f, at],
            send_sem=pair_send.at[0], recv_sem=pair_recv.at[d, f, part],
            device_id={"epoch": partner}, device_id_type=MESH,
        )

    def far_rows(f):
        return slice(NEAR if f == LATER else 2 * NEAR, OVER)

    center_rows, edge_rows = slice(OVER, OVER + center), slice(OVER + center, OVER + rows)

    def far_copy(d, f, part, short=False):
        at = (slice(2 * NEAR, OVER) if short else far_rows(f), center_rows, edge_rows)[part]
        return pltpu.make_async_remote_copy(
            src_ref=own.at[d, f, at], dst_ref=far_in.at[d - 1, f, at],
            send_sem=far_send.at[d - 1, f], recv_sem=far_recv.at[d - 1, f, part],
            device_id={"epoch": 2 * lax.rem(group + d, groups) + core}, device_id_type=MESH,
        )

    def over_copy(d, act):
        @pl.when(row > 0)
        def _():
            act(far_copy(d, LATER, 0))

        @pl.when(row == 0)
        def _():
            act(far_copy(d, LATER, 0, True))

    def cross_copy(d):
        return pltpu.make_async_remote_copy(
            src_ref=pair_out.at[d, FIRST, far_rows(FIRST)], dst_ref=cross_in.at[d - 1],
            send_sem=cross_send.at[d - 1], recv_sem=cross_recv.at[d - 1],
            device_id={"epoch": 2 * lax.rem(group + d, groups) + 1 - core}, device_id_type=MESH,
        )

    neighbours = ((row > 0, row - 1), (row < row_devices - 1, row + 1))

    def near_copy(d, f, way):
        return pltpu.make_async_remote_copy(
            src_ref=near_out.at[way, d, f], dst_ref=near_in.at[way, d, f],
            send_sem=near_send.at[way], recv_sem=near_recv.at[way, d, f],
            device_id={"row": neighbours[way][1]}, device_id_type=MESH,
        )

    def row_copy(f, way):
        if f == LATER and way == 0:
            return pltpu.make_async_remote_copy(
                src_ref=up_out, dst_ref=up_in, send_sem=up_send.at[0], recv_sem=row_recv.at[0, f],
                device_id={"row": neighbours[0][1]}, device_id_type=MESH,
            )
        return pltpu.make_async_remote_copy(
            src_ref=row_out.at[way, f], dst_ref=row_in.at[way, f],
            send_sem=row_send.at[way], recv_sem=row_recv.at[way, f],
            device_id={"row": neighbours[way][1]}, device_id_type=MESH,
        )

    def near_ways(f):
        return (1,) if f == LATER else (0, 1)

    def to_neighbours(copy_of, *which, ways=(0, 1)):
        for way in ways:
            @pl.when(neighbours[way][0])
            def _():
                copy_of(*which, way).start()

    def from_neighbours(copy_of, which, add, ways=(0, 1)):
        for way in ways:
            @pl.when(neighbours[1 - way][0])
            def _():
                copy_of(*which, way).wait_recv()
                add(way)

    def finish(d, f):
        pair_copy(d, f, 0).wait_recv()
        total = own[d, f, :OVER] + pair_in[d, f, :OVER]
        if not d or f == LATER:
            own[d, f, NEAR:OVER] = total[NEAR:]
        if d and f == LATER:
            over_copy(d, lambda copy: copy.start())
        for way in near_ways(f):
            at = (1 - way) * NEAR
            near_out[way, d, f] = total[at : at + PAD]
        to_neighbours(near_copy, d, f, ways=near_ways(f))
        pair_copy(d, f, 1).wait_recv()
        own[d, f, OVER:] = own[d, f, OVER:] + pair_in[d, f, OVER:]
        if d:
            far_copy(d, f, 1).start()

    def finish_edges(d, f):
        def add(way):
            at = slice(OVER + rows - PAD, OVER + rows) if way == 0 else slice(OVER + center, OVER + center + PAD)
            own[d, f, at] = own[d, f, at] + near_in[way, d, f]

        from_neighbours(near_copy, (d, f), add, near_ways(f))
        far_copy(d, f, 2).start()

    def pair_of(d):
        goal = 2 * lax.rem(group + d, groups)
        return goal + 1 - core, goal + core

    order = (*range(1, groups), 0)
    items = [(d, f) for d in order for f in FIELDS]
    matrices = [row_matrices(v) for v in pair_of(order[0])]
    for n, (d, f) in enumerate(items):
        pair = pair_of(d)
        if n < 2:
            for copy in loads[:2] if n == 0 else loads[2:]:
                copy.wait()
            for e in range(epochs):
                prepare(e, f)
            for e in range(epochs):
                convolve(e, f)
        elif f == FIRST:
            matrices = [row_matrices(v) for v in pair]
        for h in range(2):
            columns_stage(h, pair[h], f)
        part, own_part = (rows_stage(h, matrices[h][f]) for h in range(2))
        own[d, f] = own_part[: OVER + rows]
        if n == 0:
            above = lax.div(row + row_devices - 1, row_devices)
            below = lax.div(2 * row_devices - 2 - row, row_devices)
            pl.semaphore_wait(barrier, 2 * groups - 1 + above + below)
        pair_out[d, f] = part[: OVER + rows]
        for part in range(2):
            pair_copy(d, f, part).start()
        if d and f == FIRST:
            far_copy(d, f, 0).start()
            cross_copy(d).start()
        if n == 1:
            finish(*items[0])
        if n > 2:
            finish(*items[n - 2])
    for item in items[-2:]:
        finish(*item)
    upward = rates[0, me] >= 0
    for d in range(1, groups):
        finish_edges(d, FIRST)
    for f in FIELDS:
        far = own[0, f, far_rows(f)]
        for d in range(1, groups):
            if f == LATER:
                over_copy(d, lambda copy: copy.wait_recv())
            else:
                far_copy(d, f, 0).wait_recv()
            far = far + far_in[d - 1, f, far_rows(f)]
            if f == FIRST:
                cross_copy(d).wait_recv()
                far = far + cross_in[d - 1]
        if f == LATER:
            up_out[NEAR:] = far[:PAD]
            far = far[NEAR:]
            up_out[:NEAR] = jnp.where(upward, far, 0.0)
        else:
            row_out[0, f] = jnp.where(upward, far, 0.0)
        row_out[1, f] = jnp.where(upward, 0.0, far)
        to_neighbours(row_copy, f)

    for d in range(1, groups):
        finish_edges(d, LATER)

    def add_to(f, at, value):
        out[f, at] = out[f, at] + value

    for f in FIELDS:
        total = own[0, f, OVER:]
        out[f, NEAR : rows - NEAR] = total[:center]
        out[f, :NEAR] = total[center : center + NEAR]
        out[f, rows - NEAR :] = total[center + NEAR :]
        from_neighbours(near_copy, (0, f), lambda way: add_to(
            f, slice(rows - PAD, rows) if way == 0 else slice(0, PAD), near_in[way, 0, f]
        ), near_ways(f))
    for f in FIELDS:
        for d in range(1, groups):
            far_copy(d, f, 1).wait_recv()
            add_to(f, slice(NEAR, rows - NEAR), far_in[d - 1, f, center_rows])
    for f in FIELDS:
        def add_far(way):
            if way == 1:
                add_to(f, slice(PAD, PAD + NEAR), row_in[1, f])
            elif f == LATER:
                add_to(f, slice(rows - PAD - NEAR, rows), up_in[...])
            else:
                add_to(f, slice(rows - PAD - NEAR, rows - PAD), row_in[0, f])

        from_neighbours(row_copy, (f,), add_far)
        for d in range(1, groups):
            far_copy(d, f, 2).wait_recv()
            edges = far_in[d - 1, f, edge_rows]
            add_to(f, slice(0, NEAR), edges[:NEAR])
            add_to(f, slice(rows - NEAR, rows), edges[NEAR:])

    def wait_sent(src, sem):
        pltpu.make_async_copy(src, src, sem).wait()

    wait_sent(pair_out, pair_send.at[0])
    for d in range(1, groups):
        wait_sent(own.at[d, FIRST, 2 * NEAR :], far_send.at[d - 1, FIRST])

        @pl.when(row > 0)
        def _():
            wait_sent(own.at[d, LATER, NEAR:], far_send.at[d - 1, LATER])

        @pl.when(row == 0)
        def _():
            wait_sent(own.at[d, LATER, 2 * NEAR :], far_send.at[d - 1, LATER])


        cross_copy(d).wait_send()

    @pl.when(neighbours[0][0])
    def _():
        wait_sent(near_out.at[0, :, FIRST], near_send.at[0])
        row_copy(FIRST, 0).wait_send()
        row_copy(LATER, 0).wait_send()

    @pl.when(neighbours[1][0])
    def _():
        wait_sent(near_out.at[1], near_send.at[1])
        wait_sent(row_out.at[1], row_send.at[1])


def solution(mesh):
    epoch_devices, row_devices = mesh.shape["epoch"], mesh.shape["row"]
    groups = epoch_devices // 2

    def on_device(flux_image, inv_var, pixel_mask, psf_columns, psf_rows, epoch_times, trial_rates):
        epochs, rows, columns = flux_image.shape
        depth = epochs * rows
        assert epoch_devices % 2 == 0 and trial_rates.shape[0] == epoch_devices
        assert rows % (2 * NEAR) == 0 and rows > 2 * NEAR and columns % LANES == 0 and depth % LANES == 0
        far = max(groups - 1, 1)
        hbm = pl.BlockSpec(memory_space=pl.ANY)
        vmem = pl.BlockSpec(memory_space=pltpu.VMEM)
        image = (epochs, rows, columns)

        def buffer(*size):
            return pltpu.VMEM((*size, columns), F32)

        block = OVER + rows
        dma = pltpu.SemaphoreType.DMA
        stacks = pl.pallas_call(
            functools.partial(kernel, (groups, row_devices)),
            out_shape=pltpu.VMEM((2, rows, columns), F32),
            in_specs=[hbm] * 7,
            out_specs=vmem,
            scratch_shapes=[
                pltpu.SMEM(psf_columns.shape, F32),
                pltpu.SMEM(psf_rows.shape, F32),
                pltpu.SMEM(epoch_times.shape, jnp.int32),
                pltpu.SMEM(trial_rates.shape[::-1], jnp.int32),
                pltpu.VMEM(image, F32),
                pltpu.VMEM(image, F32),
                pltpu.VMEM(image, jnp.int32),
                pltpu.VMEM((epochs, 2, BAND, BAND), BF16),
                pltpu.VMEM((epochs, 2, 2, rows, columns + BAND), BF16),
                pltpu.VMEM((2, 2 * depth, columns + LANES), BF16),
                pltpu.VMEM((2, 2 * depth, columns), BF16),
                buffer(groups, 2, block),
                buffer(groups, 2, block),
                buffer(groups, 2, block),
                buffer(far, 2, block),
                buffer(far, NEAR),
                buffer(2, groups, 2, PAD),
                buffer(2, groups, 2, PAD),
                buffer(2, 2, NEAR),
                buffer(2, 2, NEAR),
                buffer(NEAR + PAD),
                buffer(NEAR + PAD),
                dma((4,)),
                dma((3,)),
                dma((1,)),
                dma((groups, 2, 2)),
                dma((far, 2)),
                dma((far, 2, 3)),
                dma((2,)),
                dma((2, groups, 2)),
                dma((2,)),
                dma((2, 2)),
                dma((1,)),
                dma((far,)),
                dma((far,)),
            ],
            compiler_params=pltpu.CompilerParams(collective_id=0, has_side_effects=True),
        )(flux_image, inv_var, pixel_mask, psf_columns, psf_rows, epoch_times, trial_rates.T)
        return stacks[:1], stacks[1:]

    in_specs = (
        P("epoch", "row", None),
        P("epoch", "row", None),
        P("epoch", "row", None),
        P("epoch", None),
        P("epoch", None),
        P("epoch"),
        P(),
    )
    out_specs = (P("epoch", "row", None), P("epoch", "row", None))
    return jax.shard_map(
        on_device, mesh=mesh, in_specs=in_specs, out_specs=out_specs, check_vma=False
    )
```

```python
import functools

import jax
import jax.numpy as jnp
from jax import lax
from jax.experimental import pallas as pl
from jax.experimental.pallas import tpu as pltpu
from jax.sharding import PartitionSpec as P

HALO = 8
PAD = 6
TSPAN = 64
TAPS = 2 * PAD + 1
LANES = 128
NEAR = 8
OVER = 3 * NEAR
EDGES = 2 * NEAR
BAND = 2 * LANES
FIELDS = (1, 0)
FIRST, LATER = FIELDS
MESH = pl.DeviceIdType.MESH
F32 = jnp.float32
BF16 = jnp.bfloat16


def split(x):
    high = x.astype(BF16)
    return high, (x - high.astype(F32)).astype(BF16)


def iota(shape, axis):
    return lax.broadcasted_iota(jnp.int32, shape, axis)


def kernel(
    sizes,
    flux_hbm, inv_hbm, mask_hbm, psf_columns_hbm, psf_rows_hbm, times_hbm, rates_hbm,
    out,
    psf_columns, psf_rows, times, rates,
    flux, inv, mask, toeplitz, padded, convolved, shifted,
    pair_out, pair_in, own, far_in, cross_in, near_out, near_in, row_out, row_in, up_out, up_in,
    small_sem, load_sem, pair_recv, far_send, far_recv,
    near_recv, row_recv, cross_send, cross_recv,
):
    groups, row_devices = sizes
    epochs, rows, columns = flux.shape
    tiles = columns // LANES
    depth = epochs * rows
    center = rows - EDGES
    me = lax.axis_index("epoch")
    core, group = lax.rem(me, 2), me // 2
    partner = me + 1 - 2 * core
    row = lax.axis_index("row")

    smalls = []
    for n, (src, dst) in enumerate((
        (psf_columns_hbm, psf_columns), (psf_rows_hbm, psf_rows), (times_hbm, times), (rates_hbm, rates),
    )):
        copy = pltpu.make_async_copy(src, dst, small_sem.at[n])
        copy.start()
        smalls.append(copy)
    loads = []
    for n, (src, dst) in enumerate(((inv_hbm, inv), (mask_hbm, mask), (flux_hbm, flux))):
        copy = pltpu.make_async_copy(src, dst, load_sem.at[n])
        copy.start()
        loads.append(copy)

    barrier = pltpu.get_barrier_semaphore()
    pl.semaphore_signal(barrier, inc=1, device_id={"epoch": partner}, device_id_type=MESH)
    for d in range(1, groups):
        there = 2 * lax.rem(group + d, groups)
        for c in range(2):
            pl.semaphore_signal(barrier, inc=1, device_id={"epoch": there + c}, device_id_type=MESH)

    @pl.when(row > 0)
    def _():
        pl.semaphore_signal(barrier, inc=1, device_id={"row": row - 1}, device_id_type=MESH)

    @pl.when(row < row_devices - 1)
    def _():
        pl.semaphore_signal(barrier, inc=1, device_id={"row": row + 1}, device_id_type=MESH)

    for copy in smalls:
        copy.wait()
    offset = BAND // 4 - PAD - HALO
    tall = 2 * NEAR
    place = iota((tall, LANES), 0) - iota((tall, LANES), 1)
    wrapped = lax.rem(place - offset + 4 * LANES, LANES)
    for e in range(epochs):
        plain = jnp.zeros((tall, LANES), F32)
        for tap in range(TAPS):
            plain = jnp.where(wrapped == tap, psf_columns[e, tap], plain)
        for m in range(BAND // tall):
            turned = pltpu.roll(plain, (tall * m) % LANES, 1) if (tall * m) % LANES else plain
            where = place + (tall * m - offset)
            turned = jnp.where((where >= 0) & (where < TAPS), turned, 0.0)
            for f, value in enumerate((turned, turned * turned)):
                for n, piece in enumerate(split(value)):
                    toeplitz[e, f, m * tall : (m + 1) * tall, n * LANES : (n + 1) * LANES] = piece

    def shift(v, axis, e):
        return (rates[axis, v] * times[e]) >> (TSPAN.bit_length() - 1)

    def row_matrices(v):
        shape = (OVER + rows + NEAR, depth)
        o, k = iota(shape, 0), iota(shape, 1)
        far = jnp.where(rates[0, v] >= 0, -PAD - NEAR, rows + PAD)
        r = jnp.where(o < NEAR, o + rows, o - NEAR - PAD)
        r = jnp.where(o >= 2 * NEAR, o - 2 * NEAR + far, r)
        r = jnp.where(o >= OVER, o - OVER + NEAR, r)
        r = jnp.where(o >= OVER + center, o - OVER - center, r)
        r = jnp.where(o >= OVER + rows - NEAR, o - OVER, r)
        spare = (o >= OVER + rows) | ((o >= PAD) & (o < NEAR))
        spare = spare | ((o >= NEAR + PAD) & (o < 2 * NEAR))
        epoch_of = k // rows
        step = jnp.zeros(shape, jnp.int32)
        for e in range(epochs):
            step = jnp.where(epoch_of == e, shift(v, 0, e), step)
        at = r + step
        good = (at + row * rows >= 0) & (at + row * rows < rows * row_devices) & ~spare
        tap_at = jnp.where(good, lax.rem(k, rows) - at + PAD, -1)
        one_row = epoch_of[:1]
        plain = jnp.zeros(shape, F32)
        for tap in range(TAPS):
            value = jnp.zeros((1, depth), F32)
            for e in range(epochs):
                value = jnp.where(one_row == e, psf_rows[e, tap], value)
            plain = jnp.where(tap_at == tap, value, plain)
        stacks = []
        for value in (plain, plain * plain):
            high, low = split(value)
            both = jnp.concatenate([high, low], axis=0)
            stacks.append(jnp.concatenate([both, both], axis=1))
        return stacks

    half_lane = iota((rows, LANES), 1) < LANES // 2
    lane = iota((rows, LANES), 1)

    def prepare(e, f):
        field = inv[e] * mask[e].astype(F32)
        if f == 0:
            field = flux[e] * field
        turned = pltpu.roll(field, LANES // 2, 1)
        first = turned[:, :LANES]
        for n, piece in enumerate(split(turned)):
            padded[e, f, n, :, LANES:columns] = piece[:, LANES:]
        for n, piece in enumerate(split(jnp.where(half_lane, 0.0, first))):
            padded[e, f, n, :, :LANES] = piece
        for n, piece in enumerate(split(jnp.where(half_lane, first, 0.0))):
            padded[e, f, n, :, columns : columns + LANES] = piece
            padded[e, f, n, :, columns + LANES :] = jnp.zeros((rows, LANES), BF16)

    def convolve(e, f):
        windows = [
            padded[e, f, n, :, t * LANES : t * LANES + BAND] for n in range(2) for t in range(tiles + 1)
        ]
        result = jnp.dot(
            jnp.concatenate(windows, axis=0), toeplitz[e, f], preferred_element_type=F32
        )
        middle = (tiles + 1) * rows
        result = result[:middle, :LANES] + (result[:middle, LANES:] + result[middle:, :LANES])
        for t in range(tiles + 1):
            block = result[t * rows : (t + 1) * rows]
            if t == 0:
                block = jnp.where(lane >= HALO, block, 0.0)
            if t == tiles:
                block = jnp.where(lane < HALO, block, 0.0)
            for n, piece in enumerate(split(block)):
                at = slice(n * depth + e * rows, n * depth + (e + 1) * rows)
                convolved[f, at, t * LANES : (t + 1) * LANES] = piece

    def columns_stage(h, v, f):
        for e in range(epochs):
            step = shift(v, 1, e) + HALO
            stay = lane < LANES - step
            turn = lax.rem(LANES - step, LANES)
            for n in range(2):
                at = slice(n * depth + e * rows, n * depth + (e + 1) * rows)
                turned = [
                    pltpu.roll(convolved[f, at, t * LANES : (t + 1) * LANES], turn, 1)
                    for t in range(tiles + 1)
                ]
                for t in range(tiles):
                    shifted[h, at, t * LANES : (t + 1) * LANES] = jnp.where(stay, turned[t], turned[t + 1])

    def rows_stage(h, matrix):
        result = jnp.dot(matrix, shifted[h], preferred_element_type=F32)
        half = matrix.shape[0] // 2
        return result[:half] + result[half:]

    pair_send, up_send = small_sem.at[0], load_sem.at[1]
    near_send = (small_sem.at[1], small_sem.at[2])
    row_send = (small_sem.at[3], load_sem.at[0])

    def pair_copy(d, f, part):
        at = slice(part * OVER, OVER + part * rows)
        return pltpu.make_async_remote_copy(
            src_ref=pair_out.at[d, f, at], dst_ref=pair_in.at[d, f, at],
            send_sem=pair_send, recv_sem=pair_recv.at[d, f, part],
            device_id={"epoch": partner}, device_id_type=MESH,
        )

    def far_rows(f):
        return slice(NEAR if f == LATER else 2 * NEAR, OVER)

    center_rows, edge_rows = slice(OVER, OVER + center), slice(OVER + center, OVER + rows)

    def far_copy(d, f, part, short=False):
        at = (slice(2 * NEAR, OVER) if short else far_rows(f), center_rows, edge_rows)[part]
        return pltpu.make_async_remote_copy(
            src_ref=own.at[d, f, at], dst_ref=far_in.at[d - 1, f, at],
            send_sem=far_send.at[d - 1, f], recv_sem=far_recv.at[d - 1, f, part],
            device_id={"epoch": 2 * lax.rem(group + d, groups) + core}, device_id_type=MESH,
        )

    def over_copy(d, act):
        @pl.when(row > 0)
        def _():
            act(far_copy(d, LATER, 0))

        @pl.when(row == 0)
        def _():
            act(far_copy(d, LATER, 0, True))

    def cross_copy(d):
        return pltpu.make_async_remote_copy(
            src_ref=pair_out.at[d, FIRST, far_rows(FIRST)], dst_ref=cross_in.at[d - 1],
            send_sem=cross_send.at[d - 1], recv_sem=cross_recv.at[d - 1],
            device_id={"epoch": 2 * lax.rem(group + d, groups) + 1 - core}, device_id_type=MESH,
        )

    neighbours = ((row > 0, row - 1), (row < row_devices - 1, row + 1))

    def near_copy(d, f, way):
        return pltpu.make_async_remote_copy(
            src_ref=near_out.at[way, d, f], dst_ref=near_in.at[way, d, f],
            send_sem=near_send[way], recv_sem=near_recv.at[way, d, f],
            device_id={"row": neighbours[way][1]}, device_id_type=MESH,
        )

    def row_copy(f, way):
        if f == LATER and way == 0:
            return pltpu.make_async_remote_copy(
                src_ref=up_out, dst_ref=up_in, send_sem=up_send, recv_sem=row_recv.at[0, f],
                device_id={"row": neighbours[0][1]}, device_id_type=MESH,
            )
        return pltpu.make_async_remote_copy(
            src_ref=row_out.at[way, f], dst_ref=row_in.at[way, f],
            send_sem=row_send[way], recv_sem=row_recv.at[way, f],
            device_id={"row": neighbours[way][1]}, device_id_type=MESH,
        )

    def near_ways(f):
        return (1,) if f == LATER else (0, 1)

    def to_neighbours(copy_of, *which, ways=(0, 1)):
        for way in ways:
            @pl.when(neighbours[way][0])
            def _():
                copy_of(*which, way).start()

    def from_neighbours(copy_of, which, add, ways=(0, 1)):
        for way in ways:
            @pl.when(neighbours[1 - way][0])
            def _():
                copy_of(*which, way).wait_recv()
                add(way)

    def finish(d, f):
        pair_copy(d, f, 0).wait_recv()
        total = own[d, f, :OVER] + pair_in[d, f, :OVER]
        if not d or f == LATER:
            own[d, f, NEAR:OVER] = total[NEAR:]
        if d and f == LATER:
            over_copy(d, lambda copy: copy.start())
        for way in near_ways(f):
            at = (1 - way) * NEAR
            near_out[way, d, f] = total[at : at + PAD]
        to_neighbours(near_copy, d, f, ways=near_ways(f))
        pair_copy(d, f, 1).wait_recv()
        own[d, f, OVER:] = own[d, f, OVER:] + pair_in[d, f, OVER:]
        if d:
            far_copy(d, f, 1).start()

    def finish_edges(d, f):
        def add(way):
            at = slice(OVER + rows - PAD, OVER + rows) if way == 0 else slice(OVER + center, OVER + center + PAD)
            own[d, f, at] = own[d, f, at] + near_in[way, d, f]

        from_neighbours(near_copy, (d, f), add, near_ways(f))
        far_copy(d, f, 2).start()

    def pair_of(d):
        goal = 2 * lax.rem(group + d, groups)
        return goal + 1 - core, goal + core

    order = (*range(1, groups), 0)
    items = [(d, f) for d in order for f in FIELDS]
    matrices = [row_matrices(v) for v in pair_of(order[0])]
    for n, (d, f) in enumerate(items):
        pair = pair_of(d)
        if n < 2:
            for copy in loads[:2] if n == 0 else loads[2:]:
                copy.wait()
            for e in range(epochs):
                prepare(e, f)
            for e in range(epochs):
                convolve(e, f)
        elif f == FIRST:
            matrices = [row_matrices(v) for v in pair]
        for h in range(2):
            columns_stage(h, pair[h], f)
        part, own_part = (rows_stage(h, matrices[h][f]) for h in range(2))
        own[d, f] = own_part[: OVER + rows]
        if n == 0:
            above = lax.div(row + row_devices - 1, row_devices)
            below = lax.div(2 * row_devices - 2 - row, row_devices)
            pl.semaphore_wait(barrier, 2 * groups - 1 + above + below)
        pair_out[d, f] = part[: OVER + rows]
        for part in range(2):
            pair_copy(d, f, part).start()
        if d and f == FIRST:
            far_copy(d, f, 0).start()
            cross_copy(d).start()
        if n == 1:
            finish(*items[0])
        if n > 2:
            finish(*items[n - 2])
    for item in items[-2:]:
        finish(*item)
    upward = rates[0, me] >= 0
    for d in range(1, groups):
        finish_edges(d, FIRST)
    for f in FIELDS:
        far = own[0, f, far_rows(f)]
        for d in range(1, groups):
            if f == LATER:
                over_copy(d, lambda copy: copy.wait_recv())
            else:
                far_copy(d, f, 0).wait_recv()
            far = far + far_in[d - 1, f, far_rows(f)]
            if f == FIRST:
                cross_copy(d).wait_recv()
                far = far + cross_in[d - 1]
        if f == LATER:
            up_out[NEAR:] = far[:PAD]
            far = far[NEAR:]
            up_out[:NEAR] = jnp.where(upward, far, 0.0)
        else:
            row_out[0, f] = jnp.where(upward, far, 0.0)
        row_out[1, f] = jnp.where(upward, 0.0, far)
        to_neighbours(row_copy, f)

    for d in range(1, groups):
        finish_edges(d, LATER)

    def add_to(f, at, value):
        out[f, at] = out[f, at] + value

    for f in FIELDS:
        total = own[0, f, OVER:]
        out[f, NEAR : rows - NEAR] = total[:center]
        out[f, :NEAR] = total[center : center + NEAR]
        out[f, rows - NEAR :] = total[center + NEAR :]
        from_neighbours(near_copy, (0, f), lambda way: add_to(
            f, slice(rows - PAD, rows) if way == 0 else slice(0, PAD), near_in[way, 0, f]
        ), near_ways(f))
    for f in FIELDS:
        for d in range(1, groups):
            far_copy(d, f, 1).wait_recv()
            add_to(f, slice(NEAR, rows - NEAR), far_in[d - 1, f, center_rows])
    for f in FIELDS:
        def add_far(way):
            if way == 1:
                add_to(f, slice(PAD, PAD + NEAR), row_in[1, f])
            elif f == LATER:
                add_to(f, slice(rows - PAD - NEAR, rows), up_in[...])
            else:
                add_to(f, slice(rows - PAD - NEAR, rows - PAD), row_in[0, f])

        from_neighbours(row_copy, (f,), add_far)
        for d in range(1, groups):
            far_copy(d, f, 2).wait_recv()
            edges = far_in[d - 1, f, edge_rows]
            add_to(f, slice(0, NEAR), edges[:NEAR])
            add_to(f, slice(rows - NEAR, rows), edges[NEAR:])

    def wait_sent(src, sem):
        pltpu.make_async_copy(src, src, sem).wait()

    wait_sent(pair_out, pair_send)
    for d in range(1, groups):
        wait_sent(own.at[d, FIRST, 2 * NEAR :], far_send.at[d - 1, FIRST])

        @pl.when(row > 0)
        def _():
            wait_sent(own.at[d, LATER, NEAR:], far_send.at[d - 1, LATER])

        @pl.when(row == 0)
        def _():
            wait_sent(own.at[d, LATER, 2 * NEAR :], far_send.at[d - 1, LATER])


        cross_copy(d).wait_send()

    @pl.when(neighbours[0][0])
    def _():
        wait_sent(near_out.at[0, :, FIRST], near_send[0])
        row_copy(FIRST, 0).wait_send()
        row_copy(LATER, 0).wait_send()

    @pl.when(neighbours[1][0])
    def _():
        wait_sent(near_out.at[1], near_send[1])
        wait_sent(row_out.at[1], row_send[1])


def solution(mesh):
    epoch_devices, row_devices = mesh.shape["epoch"], mesh.shape["row"]
    groups = epoch_devices // 2

    def on_device(flux_image, inv_var, pixel_mask, psf_columns, psf_rows, epoch_times, trial_rates):
        epochs, rows, columns = flux_image.shape
        depth = epochs * rows
        assert epoch_devices % 2 == 0 and trial_rates.shape[0] == epoch_devices
        assert rows % (2 * NEAR) == 0 and rows > 2 * NEAR and columns % LANES == 0 and depth % LANES == 0
        far = max(groups - 1, 1)
        hbm = pl.BlockSpec(memory_space=pl.ANY)
        vmem = pl.BlockSpec(memory_space=pltpu.VMEM)
        image = (epochs, rows, columns)

        def buffer(*size):
            return pltpu.VMEM((*size, columns), F32)

        block = OVER + rows
        dma = pltpu.SemaphoreType.DMA
        stacks = pl.pallas_call(
            functools.partial(kernel, (groups, row_devices)),
            out_shape=pltpu.VMEM((2, rows, columns), F32),
            in_specs=[hbm] * 7,
            out_specs=vmem,
            scratch_shapes=[
                pltpu.SMEM(psf_columns.shape, F32),
                pltpu.SMEM(psf_rows.shape, F32),
                pltpu.SMEM(epoch_times.shape, jnp.int32),
                pltpu.SMEM(trial_rates.shape[::-1], jnp.int32),
                pltpu.VMEM(image, F32),
                pltpu.VMEM(image, F32),
                pltpu.VMEM(image, jnp.int32),
                pltpu.VMEM((epochs, 2, BAND, BAND), BF16),
                pltpu.VMEM((epochs, 2, 2, rows, columns + BAND), BF16),
                pltpu.VMEM((2, 2 * depth, columns + LANES), BF16),
                pltpu.VMEM((2, 2 * depth, columns), BF16),
                buffer(groups, 2, block),
                buffer(groups, 2, block),
                buffer(groups, 2, block),
                buffer(far, 2, block),
                buffer(far, NEAR),
                buffer(2, groups, 2, PAD),
                buffer(2, groups, 2, PAD),
                buffer(2, 2, NEAR),
                buffer(2, 2, NEAR),
                buffer(NEAR + PAD),
                buffer(NEAR + PAD),
                dma((4,)),
                dma((3,)),
                dma((groups, 2, 2)),
                dma((far, 2)),
                dma((far, 2, 3)),
                dma((2, groups, 2)),
                dma((2, 2)),
                dma((far,)),
                dma((far,)),
            ],
            compiler_params=pltpu.CompilerParams(collective_id=0, has_side_effects=True),
        )(flux_image, inv_var, pixel_mask, psf_columns, psf_rows, epoch_times, trial_rates.T)
        return stacks[:1], stacks[1:]

    in_specs = (
        P("epoch", "row", None),
        P("epoch", "row", None),
        P("epoch", "row", None),
        P("epoch", None),
        P("epoch", None),
        P("epoch"),
        P(),
    )
    out_specs = (P("epoch", "row", None), P("epoch", "row", None))
    return jax.shard_map(
        on_device, mesh=mesh, in_specs=in_specs, out_specs=out_specs, check_vma=False
    )
```

```python
import functools

import jax
import jax.numpy as jnp
from jax import lax
from jax.experimental import pallas as pl
from jax.experimental.pallas import tpu as pltpu
from jax.sharding import PartitionSpec as P

HALO = 8
PAD = 6
TSPAN = 64
TAPS = 2 * PAD + 1
LANES = 128
NEAR = 8
OVER = 3 * NEAR
EDGES = 2 * NEAR
BAND = 2 * LANES
FIELDS = (1, 0)
FIRST, LATER = FIELDS
MESH = pl.DeviceIdType.MESH
F32 = jnp.float32
BF16 = jnp.bfloat16


def split(x):
    high = x.astype(BF16)
    return high, (x - high.astype(F32)).astype(BF16)


def iota(shape, axis):
    return lax.broadcasted_iota(jnp.int32, shape, axis)


def kernel(
    sizes,
    flux_hbm, inv_hbm, mask_hbm, psf_columns_hbm, psf_rows_hbm, times_hbm, rates_hbm,
    out,
    psf_columns, psf_rows, times, rates,
    flux, inv, mask, toeplitz, padded, convolved, shifted,
    pair_out, pair_in, own, far_in, cross_in, near_out, near_in, row_out, row_in, up_out, up_in,
    small_sem, load_sem, pair_recv, far_send, far_recv,
    near_recv, row_recv, cross_send, cross_recv,
):
    groups, row_devices = sizes
    epochs, rows, columns = flux.shape
    tiles = columns // LANES
    depth = epochs * rows
    center = rows - EDGES
    me = lax.axis_index("epoch")
    core, group = lax.rem(me, 2), me // 2
    partner = me + 1 - 2 * core
    row = lax.axis_index("row")

    smalls = []
    for n, (src, dst) in enumerate((
        (psf_columns_hbm, psf_columns), (psf_rows_hbm, psf_rows), (times_hbm, times), (rates_hbm, rates),
    )):
        copy = pltpu.make_async_copy(src, dst, small_sem.at[n])
        copy.start()
        smalls.append(copy)
    loads = []
    for n, (src, dst) in enumerate(((inv_hbm, inv), (mask_hbm, mask), (flux_hbm, flux))):
        copy = pltpu.make_async_copy(src, dst, load_sem.at[n])
        copy.start()
        loads.append(copy)

    barrier = pltpu.get_barrier_semaphore()
    pl.semaphore_signal(barrier, inc=1, device_id={"epoch": partner}, device_id_type=MESH)
    for d in range(1, groups):
        there = 2 * lax.rem(group + d, groups)
        for c in range(2):
            pl.semaphore_signal(barrier, inc=1, device_id={"epoch": there + c}, device_id_type=MESH)

    @pl.when(row > 0)
    def _():
        pl.semaphore_signal(barrier, inc=1, device_id={"row": row - 1}, device_id_type=MESH)

    @pl.when(row < row_devices - 1)
    def _():
        pl.semaphore_signal(barrier, inc=1, device_id={"row": row + 1}, device_id_type=MESH)

    for copy in smalls:
        copy.wait()
    offset = BAND // 4 - PAD - HALO
    tall = 2 * NEAR
    place = iota((tall, LANES), 0) - iota((tall, LANES), 1)
    wrapped = lax.rem(place - offset + 4 * LANES, LANES)
    for e in range(epochs):
        plain = jnp.zeros((tall, LANES), F32)
        for tap in range(TAPS):
            plain = jnp.where(wrapped == tap, psf_columns[e, tap], plain)
        for m in range(BAND // tall):
            turned = pltpu.roll(plain, (tall * m) % LANES, 1) if (tall * m) % LANES else plain
            where = place + (tall * m - offset)
            turned = jnp.where((where >= 0) & (where < TAPS), turned, 0.0)
            for f, value in enumerate((turned, turned * turned)):
                for n, piece in enumerate(split(value)):
                    toeplitz[e, f, m * tall : (m + 1) * tall, n * LANES : (n + 1) * LANES] = piece

    def shift(v, axis, e):
        return (rates[axis, v] * times[e]) >> (TSPAN.bit_length() - 1)

    def row_matrices(v):
        shape = (OVER + rows + NEAR, depth)
        o, k = iota(shape, 0), iota(shape, 1)
        far = jnp.where(rates[0, v] >= 0, -PAD - NEAR, rows + PAD)
        r = jnp.where(o < NEAR, o + rows, o - NEAR - PAD)
        r = jnp.where(o >= 2 * NEAR, o - 2 * NEAR + far, r)
        r = jnp.where(o >= OVER, o - OVER + NEAR, r)
        r = jnp.where(o >= OVER + center, o - OVER - center, r)
        r = jnp.where(o >= OVER + rows - NEAR, o - OVER, r)
        spare = (o >= OVER + rows) | ((o >= PAD) & (o < NEAR))
        spare = spare | ((o >= NEAR + PAD) & (o < 2 * NEAR))
        epoch_of = k // rows
        step = jnp.zeros(shape, jnp.int32)
        for e in range(epochs):
            step = jnp.where(epoch_of == e, shift(v, 0, e), step)
        at = r + step
        good = (at + row * rows >= 0) & (at + row * rows < rows * row_devices) & ~spare
        tap_at = jnp.where(good, lax.rem(k, rows) - at + PAD, -1)
        one_row = epoch_of[:1]
        plain = jnp.zeros(shape, F32)
        for tap in range(TAPS):
            value = jnp.zeros((1, depth), F32)
            for e in range(epochs):
                value = jnp.where(one_row == e, psf_rows[e, tap], value)
            plain = jnp.where(tap_at == tap, value, plain)
        stacks = []
        for value in (plain, plain * plain):
            high, low = split(value)
            both = jnp.concatenate([high, low], axis=0)
            stacks.append(jnp.concatenate([both, both], axis=1))
        return stacks

    half_lane = iota((rows, LANES), 1) < LANES // 2
    lane = iota((rows, LANES), 1)

    def prepare(e, f):
        field = inv[e] * mask[e].astype(F32)
        if f == 0:
            field = flux[e] * field
        turned = pltpu.roll(field, LANES // 2, 1)
        first = turned[:, :LANES]
        for n, piece in enumerate(split(turned)):
            padded[e, f, n, :, LANES:columns] = piece[:, LANES:]
        for n, piece in enumerate(split(jnp.where(half_lane, 0.0, first))):
            padded[e, f, n, :, :LANES] = piece
        for n, piece in enumerate(split(jnp.where(half_lane, first, 0.0))):
            padded[e, f, n, :, columns : columns + LANES] = piece
            padded[e, f, n, :, columns + LANES :] = jnp.zeros((rows, LANES), BF16)

    def convolve(e, f):
        windows = [
            padded[e, f, n, :, t * LANES : t * LANES + BAND] for n in range(2) for t in range(tiles + 1)
        ]
        result = jnp.dot(
            jnp.concatenate(windows, axis=0), toeplitz[e, f], preferred_element_type=F32
        )
        middle = (tiles + 1) * rows
        result = result[:middle, :LANES] + (result[:middle, LANES:] + result[middle:, :LANES])
        for t in range(tiles + 1):
            block = result[t * rows : (t + 1) * rows]
            if t == 0:
                block = jnp.where(lane >= HALO, block, 0.0)
            if t == tiles:
                block = jnp.where(lane < HALO, block, 0.0)
            for n, piece in enumerate(split(block)):
                at = slice(n * depth + e * rows, n * depth + (e + 1) * rows)
                convolved[f, at, t * LANES : (t + 1) * LANES] = piece

    def columns_stage(h, v, f):
        for e in range(epochs):
            step = shift(v, 1, e) + HALO
            stay = lane < LANES - step
            turn = lax.rem(LANES - step, LANES)
            for n in range(2):
                at = slice(n * depth + e * rows, n * depth + (e + 1) * rows)
                turned = [
                    pltpu.roll(convolved[f, at, t * LANES : (t + 1) * LANES], turn, 1)
                    for t in range(tiles + 1)
                ]
                for t in range(tiles):
                    shifted[h, at, t * LANES : (t + 1) * LANES] = jnp.where(stay, turned[t], turned[t + 1])

    def rows_stage(h, matrix):
        result = jnp.dot(matrix, shifted[h], preferred_element_type=F32)
        half = matrix.shape[0] // 2
        return result[:half] + result[half:]

    pair_send, up_send = small_sem.at[0], load_sem.at[1]
    near_send = (small_sem.at[1], small_sem.at[2])
    row_send = (small_sem.at[3], load_sem.at[0])

    def pair_copy(d, f, part):
        at = slice(part * OVER, OVER + part * rows)
        return pltpu.make_async_remote_copy(
            src_ref=pair_out.at[d, f, at], dst_ref=pair_in.at[d, f, at],
            send_sem=pair_send, recv_sem=pair_recv.at[d, f, part],
            device_id={"epoch": partner}, device_id_type=MESH,
        )

    def far_rows(f):
        return slice(NEAR if f == LATER else 2 * NEAR, OVER)

    center_rows, edge_rows = slice(OVER, OVER + center), slice(OVER + center, OVER + rows)

    def far_copy(d, f, part, short=False):
        at = (slice(2 * NEAR, OVER) if short else far_rows(f), center_rows, edge_rows)[part]
        return pltpu.make_async_remote_copy(
            src_ref=own.at[d, f, at], dst_ref=far_in.at[d - 1, f, at],
            send_sem=far_send.at[d - 1, f], recv_sem=far_recv.at[d - 1, f, part],
            device_id={"epoch": 2 * lax.rem(group + d, groups) + core}, device_id_type=MESH,
        )

    def over_copy(d, act):
        @pl.when(row > 0)
        def _():
            act(far_copy(d, LATER, 0))

        @pl.when(row == 0)
        def _():
            act(far_copy(d, LATER, 0, True))

    def cross_copy(d):
        return pltpu.make_async_remote_copy(
            src_ref=pair_out.at[d, FIRST, far_rows(FIRST)], dst_ref=cross_in.at[d - 1],
            send_sem=cross_send.at[d - 1], recv_sem=cross_recv.at[d - 1],
            device_id={"epoch": 2 * lax.rem(group + d, groups) + 1 - core}, device_id_type=MESH,
        )

    neighbours = ((row > 0, row - 1), (row < row_devices - 1, row + 1))

    def near_copy(d, f, way):
        return pltpu.make_async_remote_copy(
            src_ref=near_out.at[way, d, f], dst_ref=near_in.at[way, d, f],
            send_sem=near_send[way], recv_sem=near_recv.at[way, d, f],
            device_id={"row": neighbours[way][1]}, device_id_type=MESH,
        )

    def row_copy(f, way):
        if f == LATER and way == 0:
            return pltpu.make_async_remote_copy(
                src_ref=up_out, dst_ref=up_in, send_sem=up_send, recv_sem=row_recv.at[0, f],
                device_id={"row": neighbours[0][1]}, device_id_type=MESH,
            )
        return pltpu.make_async_remote_copy(
            src_ref=row_out.at[way, f], dst_ref=row_in.at[way, f],
            send_sem=row_send[way], recv_sem=row_recv.at[way, f],
            device_id={"row": neighbours[way][1]}, device_id_type=MESH,
        )

    def near_ways(f):
        return (1,) if f == LATER else (0, 1)

    def to_neighbours(copy_of, *which, ways=(0, 1)):
        for way in ways:
            @pl.when(neighbours[way][0])
            def _():
                copy_of(*which, way).start()

    def from_neighbours(copy_of, which, add, ways=(0, 1)):
        for way in ways:
            @pl.when(neighbours[1 - way][0])
            def _():
                copy_of(*which, way).wait_recv()
                add(way)

    def finish(d, f):
        pair_copy(d, f, 0).wait_recv()
        total = own[d, f, :OVER] + pair_in[d, f, :OVER]
        if not d or f == LATER:
            own[d, f, NEAR:OVER] = total[NEAR:]
        if d and f == LATER:
            over_copy(d, lambda copy: copy.start())
        for way in near_ways(f):
            at = (1 - way) * NEAR
            near_out[way, d, f] = total[at : at + PAD]
        to_neighbours(near_copy, d, f, ways=near_ways(f))
        pair_copy(d, f, 1).wait_recv()
        own[d, f, OVER:] = own[d, f, OVER:] + pair_in[d, f, OVER:]
        if d:
            far_copy(d, f, 1).start()

    def finish_edges(d, f):
        def add(way):
            at = slice(OVER + rows - PAD, OVER + rows) if way == 0 else slice(OVER + center, OVER + center + PAD)
            own[d, f, at] = own[d, f, at] + near_in[way, d, f]

        from_neighbours(near_copy, (d, f), add, near_ways(f))
        far_copy(d, f, 2).start()

    def pair_of(d):
        goal = 2 * lax.rem(group + d, groups)
        return goal + 1 - core, goal + core

    order = (*range(1, groups), 0)
    items = [(d, f) for d in order for f in FIELDS]
    matrices = [row_matrices(v) for v in pair_of(order[0])]
    for n, (d, f) in enumerate(items):
        pair = pair_of(d)
        if n < 2:
            for copy in loads[:2] if n == 0 else loads[2:]:
                copy.wait()
            for e in range(epochs):
                prepare(e, f)
            for e in range(epochs):
                convolve(e, f)
        elif f == FIRST:
            matrices = [row_matrices(v) for v in pair]
        for h in range(2):
            columns_stage(h, pair[h], f)
        part, own_part = (rows_stage(h, matrices[h][f]) for h in range(2))
        own[d, f] = own_part[: OVER + rows]
        if n == 0:
            above = lax.div(row + row_devices - 1, row_devices)
            below = lax.div(2 * row_devices - 2 - row, row_devices)
            pl.semaphore_wait(barrier, 2 * groups - 1 + above + below)
        pair_out[d, f] = part[: OVER + rows]
        for part in range(2):
            pair_copy(d, f, part).start()
        if d and f == FIRST:
            far_copy(d, f, 0).start()
            cross_copy(d).start()
        if n == 1:
            finish(*items[0])
        if n > 2:
            finish(*items[n - 2])
    for item in items[-2:]:
        finish(*item)
    upward = rates[0, me] >= 0
    for f in FIELDS:
        far = own[0, f, far_rows(f)]
        for d in range(1, groups):
            if f == LATER:
                over_copy(d, lambda copy: copy.wait_recv())
            else:
                far_copy(d, f, 0).wait_recv()
            far = far + far_in[d - 1, f, far_rows(f)]
            if f == FIRST:
                cross_copy(d).wait_recv()
                far = far + cross_in[d - 1]
        if f == LATER:
            up_out[NEAR:] = far[:PAD]
            far = far[NEAR:]
            up_out[:NEAR] = jnp.where(upward, far, 0.0)
        else:
            row_out[0, f] = jnp.where(upward, far, 0.0)
        row_out[1, f] = jnp.where(upward, 0.0, far)
        to_neighbours(row_copy, f)
        if f == FIRST:
            for d in range(1, groups):
                finish_edges(d, FIRST)

    for d in range(1, groups):
        finish_edges(d, LATER)

    def add_to(f, at, value):
        out[f, at] = out[f, at] + value

    for f in FIELDS:
        total = own[0, f, OVER:]
        out[f, NEAR : rows - NEAR] = total[:center]
        out[f, :NEAR] = total[center : center + NEAR]
        out[f, rows - NEAR :] = total[center + NEAR :]
        from_neighbours(near_copy, (0, f), lambda way: add_to(
            f, slice(rows - PAD, rows) if way == 0 else slice(0, PAD), near_in[way, 0, f]
        ), near_ways(f))
    for f in FIELDS:
        for d in range(1, groups):
            far_copy(d, f, 1).wait_recv()
            add_to(f, slice(NEAR, rows - NEAR), far_in[d - 1, f, center_rows])
    for f in FIELDS:
        def add_far(way):
            if way == 1:
                add_to(f, slice(PAD, PAD + NEAR), row_in[1, f])
            elif f == LATER:
                add_to(f, slice(rows - PAD - NEAR, rows), up_in[...])
            else:
                add_to(f, slice(rows - PAD - NEAR, rows - PAD), row_in[0, f])

        from_neighbours(row_copy, (f,), add_far)
        for d in range(1, groups):
            far_copy(d, f, 2).wait_recv()
            edges = far_in[d - 1, f, edge_rows]
            add_to(f, slice(0, NEAR), edges[:NEAR])
            add_to(f, slice(rows - NEAR, rows), edges[NEAR:])

    def wait_sent(src, sem):
        pltpu.make_async_copy(src, src, sem).wait()

    wait_sent(pair_out, pair_send)
    for d in range(1, groups):
        wait_sent(own.at[d, FIRST, 2 * NEAR :], far_send.at[d - 1, FIRST])

        @pl.when(row > 0)
        def _():
            wait_sent(own.at[d, LATER, NEAR:], far_send.at[d - 1, LATER])

        @pl.when(row == 0)
        def _():
            wait_sent(own.at[d, LATER, 2 * NEAR :], far_send.at[d - 1, LATER])


        cross_copy(d).wait_send()

    @pl.when(neighbours[0][0])
    def _():
        wait_sent(near_out.at[0, :, FIRST], near_send[0])
        row_copy(FIRST, 0).wait_send()
        row_copy(LATER, 0).wait_send()

    @pl.when(neighbours[1][0])
    def _():
        wait_sent(near_out.at[1], near_send[1])
        wait_sent(row_out.at[1], row_send[1])


def solution(mesh):
    epoch_devices, row_devices = mesh.shape["epoch"], mesh.shape["row"]
    groups = epoch_devices // 2

    def on_device(flux_image, inv_var, pixel_mask, psf_columns, psf_rows, epoch_times, trial_rates):
        epochs, rows, columns = flux_image.shape
        depth = epochs * rows
        assert epoch_devices % 2 == 0 and trial_rates.shape[0] == epoch_devices
        assert rows % (2 * NEAR) == 0 and rows > 2 * NEAR and columns % LANES == 0 and depth % LANES == 0
        far = max(groups - 1, 1)
        hbm = pl.BlockSpec(memory_space=pl.ANY)
        vmem = pl.BlockSpec(memory_space=pltpu.VMEM)
        image = (epochs, rows, columns)

        def buffer(*size):
            return pltpu.VMEM((*size, columns), F32)

        block = OVER + rows
        dma = pltpu.SemaphoreType.DMA
        stacks = pl.pallas_call(
            functools.partial(kernel, (groups, row_devices)),
            out_shape=pltpu.VMEM((2, rows, columns), F32),
            in_specs=[hbm] * 7,
            out_specs=vmem,
            scratch_shapes=[
                pltpu.SMEM(psf_columns.shape, F32),
                pltpu.SMEM(psf_rows.shape, F32),
                pltpu.SMEM(epoch_times.shape, jnp.int32),
                pltpu.SMEM(trial_rates.shape[::-1], jnp.int32),
                pltpu.VMEM(image, F32),
                pltpu.VMEM(image, F32),
                pltpu.VMEM(image, jnp.int32),
                pltpu.VMEM((epochs, 2, BAND, BAND), BF16),
                pltpu.VMEM((epochs, 2, 2, rows, columns + BAND), BF16),
                pltpu.VMEM((2, 2 * depth, columns + LANES), BF16),
                pltpu.VMEM((2, 2 * depth, columns), BF16),
                buffer(groups, 2, block),
                buffer(groups, 2, block),
                buffer(groups, 2, block),
                buffer(far, 2, block),
                buffer(far, NEAR),
                buffer(2, groups, 2, PAD),
                buffer(2, groups, 2, PAD),
                buffer(2, 2, NEAR),
                buffer(2, 2, NEAR),
                buffer(NEAR + PAD),
                buffer(NEAR + PAD),
                dma((4,)),
                dma((3,)),
                dma((groups, 2, 2)),
                dma((far, 2)),
                dma((far, 2, 3)),
                dma((2, groups, 2)),
                dma((2, 2)),
                dma((far,)),
                dma((far,)),
            ],
            compiler_params=pltpu.CompilerParams(collective_id=0, has_side_effects=True),
        )(flux_image, inv_var, pixel_mask, psf_columns, psf_rows, epoch_times, trial_rates.T)
        return stacks[:1], stacks[1:]

    in_specs = (
        P("epoch", "row", None),
        P("epoch", "row", None),
        P("epoch", "row", None),
        P("epoch", None),
        P("epoch", None),
        P("epoch"),
        P(),
    )
    out_specs = (P("epoch", "row", None), P("epoch", "row", None))
    return jax.shard_map(
        on_device, mesh=mesh, in_specs=in_specs, out_specs=out_specs, check_vma=False
    )
```
